32 devices in a mesh: rep: 2 (over x), seq: 16 (over z, y, core).
Axes of the slice: x: 2, y: 2, z: 4, core: 2. Of those that a mesh axis runs over, the one named last changes fastest.
Arguments:
- projected: bfloat16 [24576, 4096], P(('rep', 'seq')), parts along dimension 0, may hold values from -6 to 6
- history_in: bfloat16 [24576, 1024], P(('rep', 'seq')), parts along dimension 0, may hold values from -6 to 6
- norm_gain: float32 [1024], replicated, may hold values from 0.1 to 1.9
- out_proj: bfloat16 [1024, 1024], replicated, may hold values from -0.1875 to 0.1875
- user_spans: int32 [16], P('rep'), parts along dimension 0, may hold values from 1 to 4, as said below
- user_tails: int32 [16], P('rep'), parts along dimension 0, may hold values from 1 to 768
- cand_emb: bfloat16 [4096, 1024], P(('rep', 'seq')), parts along dimension 0, may hold values from -6 to 6
- cand_user: int32 [4096], P(('rep', 'seq')), parts along dimension 0, may hold values from 0 to 7
- cross_down: bfloat16 [2048, 128], replicated, may hold values from -0.125 to 0.125
- cross_up: bfloat16 [128, 2048], replicated, may hold values from -0.5 to 0.5
- cross_bias: float32 [2048], replicated, may hold values from -4 to 4
- score_weight: float32 [2048], replicated, may hold values from -0.125 to 0.125
Outputs:
- history_out: bfloat16 [24576, 1024], P(('rep', 'seq')), parts along dimension 0
- scores: float32 [4096], P(('rep', 'seq')), parts along dimension 0
The draws below stay inside these ranges and needn't reach their ends.
There are 2 independent parts, one for each index of `rep`. The reference program is written for one: setup_inputs(seed, part) draws one part's arguments, and reference() takes and returns one part's arrays. A program takes and returns all parts, laid end to end along the dimension named above; an argument that names none is the same for every part. Nothing has to cross between parts.
Inputs may be any that keep to these rules, and one draw needn't show every extreme that they name: `user_spans`: users own consecutive segments in order and together own all 16 segments; some user owns exactly 4.
All inputs are finite; a program needn't handle non-finite values.
Results may differ from the reference program's by a relative error of at most 0.0059.
Values may be sent and summed in bfloat16 or wider, within the bound.
A program may use at most 128 MiB of HBM per device.

```python
import jax
import jax.numpy as jnp
from jax import lax

D = 1024
HEADS = 8
RANK = 128
ROWS_DEV = 768
CAND_DEV = 128
SPAN = 4
USERS = 8
TOKENS = 12288
CANDS = 2048


def draw_user_spans(key, part):
    four_count = max(1, USERS // 8)
    three_count = USERS // 8
    one_count = 2 * four_count + three_count
    two_count = USERS - four_count - three_count - one_count
    pieces = [jnp.full((four_count,), 4, jnp.int32), jnp.full((one_count,), 1, jnp.int32)]
    if three_count > 0:
        pieces.append(jnp.full((three_count,), 3, jnp.int32))
    if two_count > 0:
        pieces.append(jnp.full((two_count,), 2, jnp.int32))
    spans = jnp.concatenate(pieces).astype(jnp.int32)
    return jax.random.permutation(jax.random.fold_in(key, 21), spans).astype(jnp.int32)


def touch_ends(result, stream_key, smallest, largest):
    spot = [jax.random.randint(jax.random.fold_in(stream_key, axis), (), 0, length) for axis, length in enumerate(result.shape)]
    longest = result.shape.index(max(result.shape))
    beside = spot[:longest] + [(spot[longest] + 1) % result.shape[longest]] + spot[longest + 1:]
    return result.at[tuple(spot)].set(smallest).at[tuple(beside)].set(largest)


def steps_of(key, shape, shards, low, top_value):
    loudness = 1.0
    for dim, blocks in shards:
        draws = jax.random.uniform(jax.random.fold_in(jax.random.fold_in(key, 6), dim), (blocks,), jnp.float32, low / len(shards), top_value / len(shards))
        loudness = loudness * jnp.repeat(jnp.exp(draws), shape[dim] // blocks).reshape((-1,) + (1,) * (len(shape) - 1 - dim))
    return loudness


def normal_values(stream_key, extent, width, reach, split=(), held_as=jnp.bfloat16):
    result = width * jax.random.normal(stream_key, extent, jnp.float32)
    if split:
        result = result * steps_of(stream_key, extent, split, -0.22, 0.18)
    return jnp.clip(result, -reach, reach).astype(held_as)


def setup_inputs(seed: int = 0, part: int = 0) -> dict:
    seeds = jax.random.split(jax.random.key(seed), 13)
    part_keys = jax.random.split(jax.random.fold_in(seeds[12], part), 13)
    return {
        "projected": normal_values(part_keys[0], (TOKENS, 4 * D), 1.0, 6.0, ((0, 16),)),
        "history_in": normal_values(part_keys[1], (TOKENS, D), 0.5, 6.0, ((0, 16),)),
        "norm_gain": jnp.clip(1.0 + 0.18 * jax.random.normal(seeds[2], (D,), jnp.float32), 0.1, 1.9),
        "out_proj": normal_values(seeds[3], (D, D), D ** -0.5, 0.1875),
        "user_spans": draw_user_spans(jax.random.fold_in(jax.random.fold_in(seeds[12], part), 71), part),
        "user_tails": touch_ends(jax.random.randint(part_keys[5], (USERS,), 1, ROWS_DEV + 1), jax.random.fold_in(part_keys[5], 1), 1, ROWS_DEV).astype(jnp.int32),
        "cand_emb": normal_values(part_keys[6], (CANDS, D), 1.0, 6.0, ((0, 16),)),
        "cand_user": touch_ends(jax.random.randint(part_keys[7], (CANDS,), 0, USERS), jax.random.fold_in(part_keys[7], 1), 0, USERS - 1).astype(jnp.int32),
        "cross_down": normal_values(seeds[8], (2 * D, RANK), (2 * D) ** -0.5, 0.125),
        "cross_up": normal_values(seeds[9], (RANK, 2 * D), RANK ** -0.5, 0.5),
        "cross_bias": normal_values(seeds[10], (2 * D,), 0.5, 4.0, (), jnp.float32),
        "score_weight": normal_values(seeds[11], (2 * D,), (2 * D) ** -0.5, 0.125, (), jnp.float32),
    }


def segment_owners(user_spans, user_tails, devices, row_count):
    last_dev = jnp.cumsum(user_spans).astype(jnp.int32) - 1
    first_dev = last_dev - user_spans.astype(jnp.int32) + 1
    device_ids = jnp.arange(devices, dtype=jnp.int32)
    owner_of = lax.optimization_barrier(jnp.sum((first_dev[None, :] <= device_ids[:, None]).astype(jnp.int32), axis=1)).astype(jnp.int32) - 1
    is_end = device_ids == last_dev[owner_of]
    valid_rows = jnp.where(is_end, user_tails[owner_of], row_count).astype(jnp.int32)
    return (last_dev, owner_of, valid_rows)

def reference(projected, history_in, norm_gain, out_proj, user_spans, user_tails, cand_emb, cand_user, cross_down, cross_up, cross_bias, score_weight):
    devices = USERS * 2
    row_count = ROWS_DEV
    model_width = D
    head_size = model_width // HEADS
    score_scale = head_size ** (-0.5)
    last_dev, owner_of, valid_rows = segment_owners(user_spans, user_tails, devices, row_count)
    blocks = projected.reshape(devices, row_count, 4 * model_width)
    residual_in = history_in.reshape(devices, row_count, model_width)
    row_ids = jnp.arange(row_count, dtype=jnp.int32)
    causal = (row_ids[None, :] <= row_ids[:, None]).astype(jnp.float32)

    def one_segment(my_index):
        own_block = blocks[my_index]
        queries = own_block[:, model_width:2 * model_width].reshape(row_count, HEADS, head_size).astype(jnp.float32)

        def attend(totals, source, weight_mask):
            key_values = blocks[source]
            key_part = key_values[:, 2 * model_width:3 * model_width].reshape(row_count, HEADS, head_size).astype(jnp.float32)
            value_part = key_values[:, 3 * model_width:].reshape(row_count, HEADS, head_size).astype(jnp.float32)
            logits = jnp.einsum('qhd,khd->hqk', queries, key_part) * score_scale
            weights = lax.optimization_barrier((jax.nn.silu(logits) * weight_mask).astype(jnp.bfloat16)).astype(jnp.float32)
            return totals + jnp.einsum('hqk,khd->qhd', weights, value_part)
        totals = attend(jnp.zeros((row_count, HEADS, head_size), jnp.float32), my_index, causal)

        def visit_block(offset, totals):
            source = (my_index - offset).astype(jnp.int32)
            clipped = jnp.maximum(source, 0).astype(jnp.int32)
            same_user = (source >= 0) & (owner_of[clipped] == owner_of[my_index])
            return lax.cond(same_user, lambda current: attend(current, clipped, jnp.float32(1.0)), lambda current: current, totals)
        totals = lax.fori_loop(1, SPAN, visit_block, totals)
        row_valid = (row_ids < valid_rows[my_index]).astype(jnp.float32)
        attention = totals.reshape(row_count, model_width) * row_valid[:, None]
        row_mean = lax.optimization_barrier(jnp.mean(attention, axis=1, keepdims=True))
        centered = attention - row_mean
        row_var = lax.optimization_barrier(jnp.mean(centered * centered, axis=1, keepdims=True))
        normed = centered * lax.rsqrt(row_var + 1e-06) * norm_gain
        gated = (normed * own_block[:, :model_width].astype(jnp.float32)).astype(jnp.bfloat16)
        return (jnp.dot(gated, out_proj, preferred_element_type=jnp.float32) + residual_in[my_index].astype(jnp.float32)).astype(jnp.bfloat16)
    history = lax.map(one_segment, jnp.arange(devices, dtype=jnp.int32))
    history_rows = history.reshape(devices * row_count, model_width)
    last_rows = (last_dev * row_count + user_tails - 1).astype(jnp.int32)
    user_rows = history_rows[last_rows]
    cand_blocks = cand_emb.reshape(devices, CAND_DEV, model_width)
    user_blocks = cand_user.reshape(devices, CAND_DEV)

    def score_block(pair):
        cand_rows, cand_users = pair
        crossed_in = jnp.concatenate([user_rows[cand_users], cand_rows], axis=1)
        low_rank = jnp.dot(crossed_in, cross_down, preferred_element_type=jnp.float32).astype(jnp.bfloat16)
        up_part = jnp.dot(low_rank, cross_up, preferred_element_type=jnp.float32)
        input_float = crossed_in.astype(jnp.float32)
        crossed = input_float * (up_part + cross_bias) + input_float
        return lax.optimization_barrier(jnp.sum(crossed * score_weight, axis=1))
    scores = lax.map(score_block, (cand_blocks, user_blocks)).reshape(devices * CAND_DEV)
    return (history_rows, scores)
```

```python
import functools

import jax
import jax.numpy as jnp
from jax import lax
from jax.experimental import pallas as pl
from jax.experimental.pallas import tpu as pltpu
from jax.sharding import PartitionSpec as P

HEADS = 8
LAG = 3
MESH = pl.DeviceIdType.MESH
OWN, PAIR = range(2)


def history_kernel(
    n, row_tile, spans_ref, tails_ref, gain_ref, proj_ref, hist_ref, weight_ref, out_ref, rows_ref,
    kv, queries, gates, residual, weights, attn, final_row, in1, in2, in3, in4, out1, out2,
    load_sem, query_sem, fill_sem, side_sem, pair_send, pair_recv, near_send, far_send, part_send, relay_send,
    recv1, recv2, recv3, recv4, row_send_sem, row_recv_sem,
):
    rep, me = lax.axis_index("rep"), lax.axis_index("seq")
    core = lax.rem(me, 2)
    side = lax.rem(me // 2, 2)
    rows, width = residual.shape
    size = width // HEADS
    half_scale = 0.5 * size ** (-0.5)
    tiles = rows // row_tile
    steps = HEADS * tiles
    partner = me + 1 - 2 * core
    even, odd = core == 0, core == 1
    slot_a, slot_b = odd & (side == 0), odd & (side == 1)

    def dev(shift):
        return lax.rem(me + shift + n, n)

    def columns(part, h):
        return pl.ds(pl.multiple_of(part * width + h * size, size), size)

    def load(h, part, target, sem):
        return pltpu.make_async_copy(proj_ref.at[:, columns(part, h)], target, sem)

    def load_queries(h, tile, target, sem):
        block = proj_ref.at[pl.ds(tile * row_tile, row_tile), columns(1, h)]
        return pltpu.make_async_copy(block, target, sem)

    def loads(h):
        return (
            load(h, 2, kv.at[OWN, h, 0], load_sem.at[h, 0]),
            load(h, 3, kv.at[OWN, h, 1], load_sem.at[h, 1]),
            *(
                load_queries(h, tile, queries.at[h * tiles + tile], query_sem.at[h * tiles + tile])
                for tile in range(tiles)
            ),
        )

    late = (
        pltpu.make_async_copy(proj_ref.at[:, pl.ds(0, width)], gates, side_sem.at[0]),
        pltpu.make_async_copy(hist_ref, residual, side_sem.at[1]),
        pltpu.make_async_copy(weight_ref, weights, side_sem.at[2]),
    )
    fills = [load_queries(s // tiles, s % tiles, out1.at[s], fill_sem.at[s]) for s in range(LAG)]
    fill_here = slot_b | (slot_a & (me + 4 >= n))

    @pl.when(fill_here)
    def _():
        for copy in fills:
            copy.start()

    @pl.loop(0, HEADS)
    def _(h):
        for copy in loads(h):
            copy.start()

    for copy in late:
        copy.start()

    barrier = pltpu.get_barrier_semaphore()

    @pl.loop(1, n)
    def _(shift):
        pl.semaphore_signal(
            barrier, inc=1, device_id=(rep, dev(shift)), device_id_type=MESH
        )

    seen = (me, me + 2, me + 4, 4 * (me // 4) + 5)

    def scan_user(user, found):
        start, last, tail, firsts = found
        end = start + spans_ref[user]
        mine = (start <= me) & (me < end)
        return (
            end,
            jnp.where(mine, end - 1, last),
            jnp.where(mine, tails_ref[user], tail),
            tuple(
                jnp.where((start <= s) & (s < end), start, first) for s, first in zip(seen, firsts)
            ),
        )

    zero = jnp.int32(0)
    _, last, tail, firsts = lax.fori_loop(
        0, spans_ref.shape[0], scan_user, (zero, zero, zero, (jnp.int32(2 * n),) * len(seen))
    )
    valid = jnp.where(me == last, tail, rows)
    first_me, first_near, first_far, first_slot = firsts
    swapped = first_slot <= 4 * (me // 4) + 3

    pl.semaphore_wait(barrier, n - 1)

    def remote(source, target, send_sem, recv_sem, device):
        return pltpu.make_async_remote_copy(
            src_ref=source,
            dst_ref=target,
            send_sem=send_sem,
            recv_sem=recv_sem,
            device_id=(rep, device),
            device_id_type=MESH,
        )

    def pair(h):
        return remote(kv.at[OWN, h], kv.at[PAIR, h], pair_send.at[h], pair_recv.at[h], partner)

    def near(s):
        return remote(queries.at[s], in1.at[s], near_send.at[s], recv1.at[s], dev(-2))

    def far(s):
        return remote(queries.at[s], in2.at[s], far_send.at[s], recv2.at[s], dev(-4))

    def far_first(s):
        return remote(queries.at[s], out1.at[s], far_send.at[s], recv2.at[s], dev(-4))

    def near_sum(s):
        return remote(out1.at[s], in3.at[s], part_send.at[s], recv3.at[s], dev(2))

    def far_sum(s):
        return remote(out2.at[s], in4.at[s], relay_send.at[s], recv4.at[s], dev(4))

    def slot(t):
        other = me + 2 - 4 * side
        return remote(out1.at[t], in1.at[t], part_send.at[t], recv1.at[t], other)

    def relay(t):
        return remote(in1.at[t], in3.at[t], relay_send.at[t], recv3.at[t], dev(4))

    @pl.loop(0, HEADS)
    def _(h):
        for copy in loads(h):
            copy.wait()
        pair(h).start()
        for tile in range(tiles):
            s = h * tiles + tile

            @pl.when(even & (me >= 2))
            def _():
                near(s).start()

            @pl.when(even & (me >= 4))
            def _():
                far(s).start()

            @pl.when(slot_a & (me >= 4))
            def _():
                @pl.when(s < LAG)
                def _():
                    far_first(s).start()

                @pl.when(s >= LAG)
                def _():
                    far(s).start()

    def weigh(q, k):
        half = half_scale * lax.dot_general(
            q, k, (((1,), (1,)), ((), ())), preferred_element_type=jnp.float32
        )
        return half + half * jnp.tanh(half)

    causal = lax.broadcasted_iota(jnp.int32, (row_tile, row_tile), 1) <= (
        lax.broadcasted_iota(jnp.int32, (row_tile, row_tile), 0)
    )

    def head_columns(h):
        return pl.ds(pl.multiple_of(h * size, size), size)

    def over(q, which, h, wanted):
        w = weigh(q, kv[which, h, 0]).astype(jnp.bfloat16)
        part = jnp.dot(w, kv[which, h, 1], preferred_element_type=jnp.float32)
        return jnp.where(wanted, part, 0.0)

    def own(h, tile):
        low, high = tile * row_tile, (tile + 1) * row_tile
        q = queries[h * tiles + tile]
        edge = jnp.where(causal, weigh(q, kv[OWN, h, 0, low:high]), 0.0).astype(jnp.bfloat16)
        total = jnp.dot(edge, kv[OWN, h, 1, low:high], preferred_element_type=jnp.float32)
        if tile:
            full = weigh(q, kv[OWN, h, 0, :low]).astype(jnp.bfloat16)
            total += jnp.dot(full, kv[OWN, h, 1, :low], preferred_element_type=jnp.float32)
        return total

    def add(h, tile, part):
        low, high = tile * row_tile, (tile + 1) * row_tile
        attn[low:high, head_columns(h)] += part.astype(jnp.float32)

    @pl.when(even)
    def _():
        @pl.loop(0, HEADS)
        def _(h):
            for tile in range(tiles):
                s = h * tiles + tile
                attn[tile * row_tile:(tile + 1) * row_tile, head_columns(h)] = own(h, tile)

                @pl.when((s >= 1) & (me + 2 < n))
                def _():
                    near_sum(s - 1).start()

                @pl.when((s >= 1) & (me + 4 < n))
                def _():
                    far_sum(s - 1).start()

                if tile == 0:
                    pair(h).wait_recv()

                @pl.when(me + 2 < n)
                def _():
                    near(s).wait_recv()
                    q = in1[s]
                    total = over(q, OWN, h, first_near <= me)
                    total += over(q, PAIR, h, first_near <= me + 1)
                    out1[s] = total.astype(jnp.bfloat16)

                @pl.when(me + 4 < n)
                def _():
                    far(s).wait_recv()
                    out2[s] = over(in2[s], PAIR, h, first_far <= me + 1).astype(jnp.bfloat16)

        @pl.when(me + 2 < n)
        def _():
            near_sum(steps - 1).start()

        @pl.when(me + 4 < n)
        def _():
            far_sum(steps - 1).start()

        @pl.when(me >= 4)
        def _():
            @pl.loop(0, HEADS)
            def _(h):
                for tile in range(tiles):
                    far_sum(h * tiles + tile).wait_recv()
                    add(h, tile, in4[h * tiles + tile])

        @pl.when(me >= 2)
        def _():
            @pl.loop(0, HEADS)
            def _(h):
                for tile in range(tiles):
                    near_sum(h * tiles + tile).wait_recv()
                    add(h, tile, in3[h * tiles + tile])

    @pl.when(odd)
    def _():
        @pl.when(fill_here)
        def _():
            for copy in fills:
                copy.wait()

        @pl.when(slot_a & (me + 4 < n))
        def _():
            for s in range(LAG):
                far_first(s).wait_recv()

        for t in range(LAG):
            slot(t).start()

        def pass_on(t):
            slot(t).wait_recv()

            @pl.when((side == 0) & (me + 4 < n))
            def _():
                relay(t).start()

        @pl.loop(0, HEADS)
        def _(h):
            for tile in range(tiles):
                t = h * tiles + tile
                if tile == 0:
                    pair(h).wait_recv()
                attn[tile * row_tile:(tile + 1) * row_tile, head_columns(h)] = own(h, tile) + over(
                    queries[t], PAIR, h, first_me <= me - 1
                )

                @pl.when(t >= 1)
                def _():
                    slot(t + LAG - 1).start()

                pass_on(t)
                q = in1[t]
                total = over(q, OWN, h, first_near <= me)
                total += over(q, PAIR, h, first_near <= me - 1)
                out1[t + LAG] = total.astype(jnp.bfloat16)

                @pl.when((t + LAG < steps) & (side == 1))
                def _():
                    out1[t + LAG] = jnp.where(swapped, out1[t + LAG], queries[t + LAG])

                @pl.when((t + LAG < steps) & (side == 0) & (me + 4 < n))
                def _():
                    far(t + LAG).wait_recv()
                    out1[t + LAG] = jnp.where(swapped, in2[t + LAG], out1[t + LAG])

        slot(steps + LAG - 1).start()

        @pl.loop(steps, steps + LAG)
        def _(t):
            pass_on(t)

        mine = first_me <= me - 2

        @pl.when(side == 1)
        def _():
            @pl.loop(0, HEADS)
            def _(h):
                for tile in range(tiles):
                    add(h, tile, jnp.where(mine, in1[h * tiles + tile + LAG], 0.0))

        @pl.when((side == 0) & (me >= 4))
        def _():
            for t in range(LAG):
                relay(t).wait_recv()

            @pl.loop(0, HEADS)
            def _(h):
                for tile in range(tiles):
                    t = h * tiles + tile + LAG
                    relay(t).wait_recv()
                    add(h, tile, jnp.where(mine, in3[t], 0.0))

    for copy in late:
        copy.wait()
    gain = gain_ref[...]

    def finish(x, gate, rest):
        centered = x - jnp.mean(x, axis=1, keepdims=True)
        var = jnp.mean(centered * centered, axis=1, keepdims=True)
        normed = centered * lax.rsqrt(var + 1e-06) * gain
        gated = (normed * gate.astype(jnp.float32)).astype(jnp.bfloat16)
        out = jnp.dot(gated, weights[...], preferred_element_type=jnp.float32)
        return (out + rest.astype(jnp.float32)).astype(jnp.bfloat16)

    final = jnp.clip(valid - 1, 0, rows - 1)
    at_last = lax.broadcasted_iota(jnp.int32, (16, rows), 1) == final
    pick = jnp.where(at_last, 1.0, 0.0).astype(jnp.bfloat16)
    picked = finish(
        jnp.broadcast_to(attn[pl.ds(final, 1), :], (16, width)),
        jnp.dot(pick, gates[...], preferred_element_type=jnp.float32),
        jnp.dot(pick, residual[...], preferred_element_type=jnp.float32),
    ).astype(jnp.float32)[0:1]
    final_row[...] = picked
    rows_ref[me] = picked

    def row_to(shift):
        return pltpu.make_async_remote_copy(
            src_ref=final_row,
            dst_ref=rows_ref.at[me],
            send_sem=row_send_sem.at[shift],
            recv_sem=row_recv_sem.at[shift],
            device_id=(rep, dev(shift)),
            device_id_type=MESH,
        )

    for tile in range(tiles):
        low, high = tile * row_tile, (tile + 1) * row_tile
        ids = low + lax.broadcasted_iota(jnp.int32, (row_tile, 1), 0)
        x = jnp.where(ids < valid, attn[low:high], 0.0)
        out_ref[low:high] = finish(x, gates[low:high], residual[low:high])
        if tile == 0:

            @pl.loop(1, n)
            def _(shift):
                row_to(shift).start()

    @pl.loop(1, n)
    def _(shift):
        row_to(shift).wait_send()
        row_to(shift).wait_recv()

    @pl.loop(0, HEADS)
    def _(h):
        pair(h).wait_send()

    @pl.loop(0, steps)
    def _(s):
        @pl.when(even & (me >= 2))
        def _():
            near(s).wait_send()

        @pl.when((even | slot_a) & (me >= 4))
        def _():
            far(s).wait_send()

        @pl.when(even & (me + 2 < n))
        def _():
            near_sum(s).wait_send()

        @pl.when(even & (me + 4 < n))
        def _():
            far_sum(s).wait_send()

    @pl.when(odd)
    def _():
        @pl.loop(0, steps + LAG)
        def _(t):
            slot(t).wait_send()

            @pl.when((side == 0) & (me + 4 < n))
            def _():
                relay(t).wait_send()


def history_layer(n, spans, tails, gain, projected, history_in, out_proj):
    rows, width = history_in.shape
    size = width // HEADS
    row_tile = next(t for t in (384, 256, 128, 64, 32, 16, rows) if rows % t == 0)
    steps = HEADS * (rows // row_tile)
    slots = steps + LAG
    smem = pl.BlockSpec(memory_space=pltpu.SMEM)
    anywhere = pl.BlockSpec(memory_space=pl.ANY)
    vmem = pl.BlockSpec(memory_space=pltpu.VMEM)
    blocks = lambda count: pltpu.VMEM((count, row_tile, size), jnp.bfloat16)
    dma = lambda *shape: pltpu.SemaphoreType.DMA(shape)
    return pl.pallas_call(
        functools.partial(history_kernel, n, row_tile),
        out_shape=(
            jax.ShapeDtypeStruct((rows, width), jnp.bfloat16),
            jax.ShapeDtypeStruct((n, 1, width), jnp.float32),
        ),
        in_specs=[smem, smem, vmem, anywhere, anywhere, anywhere],
        out_specs=(vmem, vmem),
        scratch_shapes=[
            pltpu.VMEM((2, HEADS, 2, rows, size), jnp.bfloat16),
            blocks(steps),
            pltpu.VMEM((rows, width), jnp.bfloat16),
            pltpu.VMEM((rows, width), jnp.bfloat16),
            pltpu.VMEM((width, width), jnp.bfloat16),
            pltpu.VMEM((rows, width), jnp.float32),
            pltpu.VMEM((1, width), jnp.float32),
            blocks(slots),
            blocks(steps),
            blocks(slots),
            blocks(steps),
            blocks(slots),
            blocks(steps),
            dma(HEADS, 2),
            dma(steps),
            dma(LAG),
            dma(3),
            dma(HEADS),
            dma(HEADS),
            dma(steps),
            dma(steps),
            dma(slots),
            dma(slots),
            dma(slots),
            dma(steps),
            dma(slots),
            dma(steps),
            dma(n),
            dma(n),
        ],
        compiler_params=pltpu.CompilerParams(
            collective_id=0, has_side_effects=True, vmem_limit_bytes=60 * 1024 * 1024
        ),
        name="history_layer",
    )(spans, tails, gain, projected, history_in, out_proj)


def body(
    projected,
    history_in,
    norm_gain,
    out_proj,
    user_spans,
    user_tails,
    cand_emb,
    cand_user,
    cross_down,
    cross_up,
    cross_bias,
    score_weight,
):
    model_width = history_in.shape[1]
    devices = lax.axis_size("seq")
    history_out, user_rows = history_layer(
        devices, user_spans, user_tails, norm_gain[None, :], projected, history_in, out_proj
    )
    user_rows = user_rows.reshape(devices, model_width).astype(jnp.bfloat16)
    device_ids = jnp.arange(devices, dtype=jnp.int32)
    user_count = user_spans.shape[0]
    users = jnp.arange(user_count, dtype=jnp.int32)
    last_dev = jnp.sum(jnp.where(users[None, :] <= users[:, None], user_spans[None, :], 0), axis=1) - 1
    user_match = cand_user[:, None] == jnp.arange(user_count, dtype=jnp.int32)[None, :]
    cand_dev = jnp.sum(jnp.where(user_match, last_dev[None, :], 0), axis=1)
    selector = (cand_dev[:, None] == device_ids[None, :]).astype(jnp.bfloat16)
    user_part = jnp.dot(selector, user_rows, preferred_element_type=jnp.float32).astype(
        jnp.bfloat16
    )
    crossed_in = jnp.concatenate([user_part, cand_emb], axis=1)
    low_rank = jnp.dot(crossed_in, cross_down, preferred_element_type=jnp.float32).astype(
        jnp.bfloat16
    )
    up_part = jnp.dot(low_rank, cross_up, preferred_element_type=jnp.float32)
    input_float = crossed_in.astype(jnp.float32)
    crossed = input_float * (up_part + cross_bias) + input_float
    scores = jnp.sum(crossed * score_weight, axis=1)
    return (history_out, scores)


def solution(mesh):
    in_specs = (
        P(("rep", "seq"), None),
        P(("rep", "seq"), None),
        P(),
        P(),
        P("rep"),
        P("rep"),
        P(("rep", "seq"), None),
        P(("rep", "seq")),
        P(),
        P(),
        P(),
        P(),
    )
    out_specs = (P(("rep", "seq"), None), P(("rep", "seq")))
    return jax.shard_map(body, mesh=mesh, in_specs=in_specs, out_specs=out_specs, check_vma=False)
```

```python
import functools

import jax
import jax.numpy as jnp
from jax import lax
from jax.experimental import pallas as pl
from jax.experimental.pallas import tpu as pltpu
from jax.sharding import PartitionSpec as P

HEADS = 8
LAG = 3
MESH = pl.DeviceIdType.MESH
OWN, PAIR = range(2)
TO_PAIR, TO_NEAR, TO_FAR, PART, RELAY, PASS, ROW = range(7)
QUERIES, FILLS, GATES, RESIDUAL, WEIGHTS, ROWS, OUT = range(7)


def history_kernel(
    n, row_tile, spans_ref, tails_ref, gain_ref, proj_ref, hist_ref, weight_ref, out_ref, rows_ref,
    kv, queries, gates, residual, weights, attn, final_row, in1, in2, in3, in4, in5, out1, out2,
    rows_in, out_tile, last_query, asked, answers, answer, answered,
    load_sem, once_sem, send_sem, pair_recv, recv1, recv2, recv3, recv4, recv5,
    ask_send, ask_recv, answer_send, answer_recv,
):
    rep, me = lax.axis_index("rep"), lax.axis_index("seq")
    core = lax.rem(me, 2)
    side = lax.rem(me // 2, 2)
    rows, width = residual.shape
    size = width // HEADS
    half_scale = 0.5 * size ** (-0.5)
    tiles = rows // row_tile
    steps = HEADS * tiles
    partner = me + 1 - 2 * core
    even, odd = core == 0, core == 1
    slot_a, slot_b = odd & (side == 0), odd & (side == 1)

    def dev(shift):
        return lax.rem(me + shift + n, n)

    def columns(part, h):
        return pl.ds(pl.multiple_of(part * width + h * size, size), size)

    def load(h, part, target, sem):
        return pltpu.make_async_copy(proj_ref.at[:, columns(part, h)], target, sem)

    def load_queries(h, tile, target, sem):
        block = proj_ref.at[pl.ds(tile * row_tile, row_tile), columns(1, h)]
        return pltpu.make_async_copy(block, target, sem)

    def loads(h):
        return (
            load(h, 2, kv.at[OWN, h, 0], load_sem.at[h]),
            load(h, 3, kv.at[OWN, h, 1], load_sem.at[h]),
        )

    def query_load(h, tile):
        s = tile * HEADS + h
        return load_queries(h, tile, queries.at[s], once_sem.at[QUERIES])

    late = (
        pltpu.make_async_copy(proj_ref.at[:, pl.ds(0, width)], gates, once_sem.at[GATES]),
        pltpu.make_async_copy(hist_ref, residual, once_sem.at[RESIDUAL]),
        pltpu.make_async_copy(weight_ref, weights, once_sem.at[WEIGHTS]),
    )
    fills = [load_queries(s % HEADS, s // HEADS, out1.at[s], once_sem.at[FILLS]) for s in range(LAG)]
    fill_here = slot_b | (slot_a & (me + 4 >= n))

    @pl.when(fill_here)
    def _():
        for copy in fills:
            copy.start()

    for tile in range(tiles):
        @pl.loop(0, HEADS)
        def _(h):
            query_load(h, tile).start()

    @pl.loop(0, HEADS)
    def _(h):
        for copy in loads(h):
            copy.start()

    for copy in late:
        copy.start()

    asked[...] = jnp.zeros_like(asked)
    answered[...] = jnp.zeros_like(answered)

    barrier = pltpu.get_barrier_semaphore()

    @pl.loop(1, n)
    def _(shift):
        pl.semaphore_signal(
            barrier, inc=1, device_id=(rep, dev(shift)), device_id_type=MESH
        )

    seen = (me, me + 1, me + 2, me + 3, me + 4, 4 * (me // 4) + 5)

    def scan_user(user, found):
        start, last, tail, firsts = found
        end = start + spans_ref[user]
        mine = (start <= me) & (me < end)
        return (
            end,
            jnp.where(mine, end - 1, last),
            jnp.where(mine, tails_ref[user], tail),
            tuple(
                jnp.where((start <= s) & (s < end), start, first) for s, first in zip(seen, firsts)
            ),
        )

    zero = jnp.int32(0)
    _, last, tail, firsts = lax.fori_loop(
        0, spans_ref.shape[0], scan_user, (zero, zero, zero, (jnp.int32(2 * n),) * len(seen))
    )
    valid = jnp.where(me == last, tail, rows)
    first_me, first_near, first_far, first_slot = firsts[0], firsts[2], firsts[4], firsts[5]
    final = jnp.clip(valid - 1, 0, rows - 1)
    swapped = first_slot <= 4 * (me // 4) + 3

    pl.semaphore_wait(barrier, n - 1)

    def remote(source, target, send_sem, recv_sem, device):
        return pltpu.make_async_remote_copy(
            src_ref=source,
            dst_ref=target,
            send_sem=send_sem,
            recv_sem=recv_sem,
            device_id=(rep, device),
            device_id_type=MESH,
        )

    def all_here(block, sem):
        pltpu.make_async_copy(block, block, sem).wait()

    def pair(h):
        return remote(kv.at[OWN, h], kv.at[PAIR, h], send_sem.at[TO_PAIR], pair_recv.at[h], partner)

    def near(s):
        return remote(queries.at[s], in1.at[s], send_sem.at[TO_NEAR], recv1.at[s], dev(-2))

    def far(s):
        return remote(queries.at[s], in2.at[s], send_sem.at[TO_FAR], recv2.at[s], dev(-4))

    def across(s):
        return remote(queries.at[s], in5.at[s], send_sem.at[TO_NEAR], recv5.at[s], dev(2))

    def onward(s):
        return remote(in5.at[s], in1.at[s], send_sem.at[PASS], recv1.at[s], dev(-4))

    def far_first(s):
        return remote(queries.at[s], out1.at[s], send_sem.at[TO_FAR], recv2.at[s], dev(-4))

    def near_sum(s):
        return remote(out1.at[s], in3.at[s], send_sem.at[PART], recv3.at[s // HEADS], dev(2))

    def far_sum(s):
        return remote(out2.at[s], in4.at[s], send_sem.at[RELAY], recv4.at[s // HEADS], dev(4))

    def slot(t):
        other = me + 2 - 4 * side
        return remote(out1.at[t], in1.at[t], send_sem.at[PART], recv1.at[t], other)

    def relay(t):
        return remote(in1.at[t], in3.at[t], send_sem.at[RELAY], recv3.at[jnp.maximum(t - LAG, 0) // HEADS], dev(4))

    def ask(back):
        return remote(last_query, asked.at[back], ask_send.at[back], ask_recv.at[back], dev(-back))

    def reply(ahead):
        return remote(answer.at[ahead], answered.at[ahead], answer_send.at[ahead], answer_recv.at[ahead], dev(ahead))

    def row_to(shift):
        return remote(final_row, rows_in.at[me], send_sem.at[ROW], once_sem.at[ROWS], dev(shift))

    def at_last(low, count):
        hit = low + lax.broadcasted_iota(jnp.int32, (16, count), 1) == final
        return jnp.where(hit, 1.0, 0.0).astype(jnp.bfloat16)

    all_here(queries, once_sem.at[QUERIES])

    def send_queries(begin, end):
        @pl.loop(begin, end)
        def _(s):
            @pl.when(even & (side == 1))
            def _():
                near(s).start()

            @pl.when(even & (side == 0) & (me >= 4))
            def _():
                across(s).start()
                far(s).start()

            @pl.when(slot_a & (me >= 4))
            def _():
                @pl.when(s < LAG)
                def _():
                    far_first(s).start()

                @pl.when(s >= LAG)
                def _():
                    far(s).start()

    send_queries(0, 2)

    @pl.loop(0, HEADS)
    def _(h):
        row = sum(
            jnp.dot(
                at_last(tile * row_tile, row_tile), queries[tile * HEADS + h],
                preferred_element_type=jnp.float32,
            )
            for tile in range(tiles)
        )
        last_query[:, pl.ds(pl.multiple_of(h * size, size), size)] = row[0:1]

    asked[0] = last_query[...]

    @pl.loop(0, HEADS)
    def _(h):
        all_here(kv.at[OWN, h], load_sem.at[h])
        pair(h).start()

    for back in (1, 2, 3):
        pl.when(me >= back)(ask(back).start)

    send_queries(2, steps)

    def weigh(q, k):
        half = half_scale * lax.dot_general(
            q, k, (((1,), (1,)), ((), ())), preferred_element_type=jnp.float32
        )
        return half + half * jnp.tanh(half)

    causal = lax.broadcasted_iota(jnp.int32, (row_tile, row_tile), 1) <= (
        lax.broadcasted_iota(jnp.int32, (row_tile, row_tile), 0)
    )

    def head_columns(h):
        return pl.ds(pl.multiple_of(h * size, size), size)

    def over(q, which, h, wanted):
        w = weigh(q, kv[which, h, 0]).astype(jnp.bfloat16)
        part = jnp.dot(w, kv[which, h, 1], preferred_element_type=jnp.float32)
        return jnp.where(wanted, part, 0.0)

    def ask_phase(at):
        @pl.when(at == 2)
        def _():
            for ahead in (1, 2, 3):
                pl.when(me + ahead < n)(ask(ahead).wait_recv)
            visible = (lax.broadcasted_iota(jnp.int32, (8, rows), 0) > 0) | (
                lax.broadcasted_iota(jnp.int32, (8, rows), 1) <= final
            )

            @pl.loop(0, HEADS)
            def _(h):
                q = asked[:, 0, head_columns(h)].astype(jnp.bfloat16)
                w = jnp.where(visible, weigh(q, kv[OWN, h, 0]), 0.0).astype(jnp.bfloat16)
                answers[:, head_columns(h)] = jnp.dot(
                    w, kv[OWN, h, 1], preferred_element_type=jnp.float32
                )

            for ahead in (1, 2, 3):
                answer[ahead] = jnp.where(firsts[ahead] <= me, answers[ahead:ahead + 1], 0.0)

        @pl.when(at == 3)
        def _():
            for ahead in (1, 2, 3):
                pl.when(me + ahead < n)(reply(ahead).start)

    gain = gain_ref[...]

    def finish(x, gate, rest):
        centered = x - jnp.mean(x, axis=1, keepdims=True)
        var = jnp.mean(centered * centered, axis=1, keepdims=True)
        normed = centered * lax.rsqrt(var + 1e-06) * gain
        gated = (normed * gate.astype(jnp.float32)).astype(jnp.bfloat16)
        out = jnp.dot(gated, weights[...], preferred_element_type=jnp.float32)
        return (out + rest.astype(jnp.float32)).astype(jnp.bfloat16)

    def row_phase(at):
        @pl.when(at == 0)
        def _():
            for copy in late:
                copy.wait()
            for back in (1, 2, 3):
                pl.when(me >= back)(reply(back).wait_recv)
            total = answers[0:1] + answered[1] + answered[2] + answered[3]
            pick = at_last(0, rows)
            row = finish(
                jnp.broadcast_to(total, (16, width)),
                jnp.dot(pick, gates[...], preferred_element_type=jnp.float32),
                jnp.dot(pick, residual[...], preferred_element_type=jnp.float32),
            ).astype(jnp.float32)[0:1]
            final_row[...] = row
            rows_in[me] = row

        @pl.when(at == 1)
        def _():
            @pl.loop(1, n)
            def _(shift):
                row_to(shift).start()

    def own(h, tile):
        low, high = tile * row_tile, (tile + 1) * row_tile
        q = queries[tile * HEADS + h]
        edge = jnp.where(causal, weigh(q, kv[OWN, h, 0, low:high]), 0.0).astype(jnp.bfloat16)
        total = jnp.dot(edge, kv[OWN, h, 1, low:high], preferred_element_type=jnp.float32)
        if tile:
            full = weigh(q, kv[OWN, h, 0, :low]).astype(jnp.bfloat16)
            total += jnp.dot(full, kv[OWN, h, 1, :low], preferred_element_type=jnp.float32)
        return total

    def add(h, tile, part):
        low, high = tile * row_tile, (tile + 1) * row_tile
        attn[low:high, head_columns(h)] += part.astype(jnp.float32)

    @pl.when(even)
    def _():
        for tile in range(tiles):
            @pl.loop(0, HEADS)
            def _(h):
                s = tile * HEADS + h
                if tile == 0:
                    ask_phase(h)
                if tile == tiles - 1:
                    row_phase(h - HEADS + 2)

                @pl.when((side == 1) & (me >= 4))
                def _():
                    across(s).wait_recv()
                    onward(s).start()
                    far(s).start()

                attn[tile * row_tile:(tile + 1) * row_tile, head_columns(h)] = own(h, tile)

                @pl.when((s >= 1) & (me + 2 < n))
                def _():
                    near_sum(s - 1).start()

                @pl.when((s >= 1) & (me + 4 < n))
                def _():
                    far_sum(s - 1).start()

                if tile == 0:
                    pair(h).wait_recv()

                @pl.when(me + 2 < n)
                def _():
                    near(s).wait_recv()
                    q = in1[s]
                    total = over(q, OWN, h, first_near <= me)
                    total += over(q, PAIR, h, first_near <= me + 1)
                    out1[s] = total.astype(jnp.bfloat16)

                @pl.when(me + 4 < n)
                def _():
                    far(s).wait_recv()
                    out2[s] = over(in2[s], PAIR, h, first_far <= me + 1).astype(jnp.bfloat16)

        @pl.when(me + 2 < n)
        def _():
            near_sum(steps - 1).start()

        @pl.when(me + 4 < n)
        def _():
            far_sum(steps - 1).start()

    @pl.when(odd)
    def _():
        @pl.when(fill_here)
        def _():
            all_here(out1.at[pl.ds(0, LAG)], once_sem.at[FILLS])

        @pl.when(slot_a & (me + 4 < n))
        def _():
            for s in range(LAG):
                far_first(s).wait_recv()

        for t in range(LAG):
            slot(t).start()

        def pass_on(t):
            slot(t).wait_recv()

            @pl.when((side == 0) & (me + 4 < n))
            def _():
                relay(t).start()

        for tile in range(tiles):
            @pl.loop(0, HEADS)
            def _(h):
                t = tile * HEADS + h
                if tile == 0:
                    pair(h).wait_recv()
                    ask_phase(h)
                if tile == tiles - 1:
                    row_phase(h - HEADS // 2)
                attn[tile * row_tile:(tile + 1) * row_tile, head_columns(h)] = own(h, tile) + over(
                    queries[t], PAIR, h, first_me <= me - 1
                )

                @pl.when(t >= 1)
                def _():
                    slot(t + LAG - 1).start()

                pass_on(t)
                q = in1[t]
                total = over(q, OWN, h, first_near <= me)
                total += over(q, PAIR, h, first_near <= me - 1)
                out1[t + LAG] = total.astype(jnp.bfloat16)

                @pl.when((t + LAG < steps) & (side == 1))
                def _():
                    out1[t + LAG] = jnp.where(swapped, out1[t + LAG], queries[t + LAG])

                @pl.when((t + LAG < steps) & (side == 0) & (me + 4 < n))
                def _():
                    far(t + LAG).wait_recv()
                    out1[t + LAG] = jnp.where(swapped, in2[t + LAG], out1[t + LAG])

        slot(steps + LAG - 1).start()

        @pl.loop(steps, steps + LAG)
        def _(t):
            pass_on(t)

    mine = first_me <= me - 2

    def gather(tile):
        @pl.when(even & (me >= 4))
        def _():
            all_here(in4.at[pl.ds(tile * HEADS, HEADS)], recv4.at[tile])

            @pl.loop(0, HEADS)
            def _(h):
                add(h, tile, in4[tile * HEADS + h])

        @pl.when(even & (me >= 2))
        def _():
            all_here(in3.at[pl.ds(tile * HEADS, HEADS)], recv3.at[tile])

            @pl.loop(0, HEADS)
            def _(h):
                add(h, tile, in3[tile * HEADS + h])

        @pl.when(slot_b)
        def _():
            @pl.loop(0, HEADS)
            def _(h):
                add(h, tile, jnp.where(mine, in1[tile * HEADS + h + LAG], 0.0))

        @pl.when(slot_a & (me >= 4))
        def _():
            if tile == 0:
                all_here(in3.at[pl.ds(0, HEADS + LAG)], recv3.at[0])
            else:
                all_here(in3.at[pl.ds(tile * HEADS + LAG, HEADS)], recv3.at[tile])

            @pl.loop(0, HEADS)
            def _(h):
                add(h, tile, jnp.where(mine, in3[tile * HEADS + h + LAG], 0.0))

    def write(low, high, sem):
        return pltpu.make_async_copy(out_tile.at[pl.ds(low, high - low)], out_ref.at[pl.ds(low, high - low)], sem)

    parts = [(tile * row_tile, (tile + 1) * row_tile) for tile in range(tiles - 1)]
    cut = (tiles - 1) * row_tile + row_tile // 2 // 16 * 16
    parts += [(low, high) for low, high in (((tiles - 1) * row_tile, cut), (cut, rows)) if low < high]

    def close(part):
        low, high = parts[part]
        ids = low + lax.broadcasted_iota(jnp.int32, (high - low, 1), 0)
        x = jnp.where(ids < valid, attn[low:high], 0.0)
        out_tile[low:high] = finish(x, gates[low:high], residual[low:high])
        write(low, high, once_sem.at[OUT]).start()

    for tile in range(tiles - 1):
        gather(tile)
        close(tile)
    gather(tiles - 1)

    for part in range(tiles - 1, len(parts)):
        close(part)

    all_here(kv.at[OWN], send_sem.at[TO_PAIR])

    @pl.when(even & ((side == 1) | (me >= 4)))
    def _():
        all_here(queries, send_sem.at[TO_NEAR])

    @pl.when((even | slot_a) & (me >= 4))
    def _():
        all_here(queries, send_sem.at[TO_FAR])

    @pl.when(even & (side == 1) & (me >= 4))
    def _():
        all_here(in5, send_sem.at[PASS])

    @pl.when(even & (me + 2 < n))
    def _():
        all_here(out1.at[pl.ds(0, steps)], send_sem.at[PART])

    @pl.when(even & (me + 4 < n))
    def _():
        all_here(out2, send_sem.at[RELAY])

    @pl.when(odd)
    def _():
        all_here(out1, send_sem.at[PART])

    @pl.when(slot_a & (me + 4 < n))
    def _():
        all_here(in1, send_sem.at[RELAY])

    for back in (1, 2, 3):
        pl.when(me >= back)(ask(back).wait_send)
        pl.when(me + back < n)(reply(back).wait_send)

    all_here(rows_in.at[pl.ds(0, n - 1)], send_sem.at[ROW])
    all_here(rows_in.at[pl.ds(0, n - 1)], once_sem.at[ROWS])
    rows_ref[...] = rows_in[:, 0, :].astype(jnp.bfloat16)

    all_here(out_tile, once_sem.at[OUT])


def history_layer(n, spans, tails, gain, projected, history_in, out_proj):
    rows, width = history_in.shape
    size = width // HEADS
    row_tile = next(t for t in (384, 256, 128, 64, 32, 16, rows) if rows % t == 0)
    steps = HEADS * (rows // row_tile)
    slots = steps + LAG
    smem = pl.BlockSpec(memory_space=pltpu.SMEM)
    anywhere = pl.BlockSpec(memory_space=pl.ANY)
    vmem = pl.BlockSpec(memory_space=pltpu.VMEM)
    blocks = lambda count: pltpu.VMEM((count, row_tile, size), jnp.bfloat16)
    dma = lambda *shape: pltpu.SemaphoreType.DMA(shape)
    return pl.pallas_call(
        functools.partial(history_kernel, n, row_tile),
        out_shape=(
            jax.ShapeDtypeStruct((rows, width), jnp.bfloat16),
            jax.ShapeDtypeStruct((n, width), jnp.bfloat16),
        ),
        in_specs=[smem, smem, vmem, anywhere, anywhere, anywhere],
        out_specs=(anywhere, vmem),
        scratch_shapes=[
            pltpu.VMEM((2, HEADS, 2, rows, size), jnp.bfloat16),
            blocks(steps),
            pltpu.VMEM((rows, width), jnp.bfloat16),
            pltpu.VMEM((rows, width), jnp.bfloat16),
            pltpu.VMEM((width, width), jnp.bfloat16),
            pltpu.VMEM((rows, width), jnp.float32),
            pltpu.VMEM((1, width), jnp.float32),
            blocks(slots),
            blocks(steps),
            blocks(slots),
            blocks(steps),
            blocks(steps),
            blocks(slots),
            blocks(steps),
            pltpu.VMEM((n, 1, width), jnp.float32),
            pltpu.VMEM((rows, width), jnp.bfloat16),
            pltpu.VMEM((1, width), jnp.float32),
            pltpu.VMEM((8, 1, width), jnp.float32),
            pltpu.VMEM((8, width), jnp.float32),
            pltpu.VMEM((4, 1, width), jnp.float32),
            pltpu.VMEM((4, 1, width), jnp.float32),
            dma(HEADS),
            dma(7),
            dma(7),
            dma(HEADS),
            dma(slots),
            dma(steps),
            dma(rows // row_tile),
            dma(rows // row_tile),
            dma(steps),
            dma(4),
            dma(4),
            dma(4),
            dma(4),
        ],
        compiler_params=pltpu.CompilerParams(
            collective_id=0, has_side_effects=True, vmem_limit_bytes=60 * 1024 * 1024
        ),
        name="history_layer",
    )(spans, tails, gain, projected, history_in, out_proj)


def body(
    projected,
    history_in,
    norm_gain,
    out_proj,
    user_spans,
    user_tails,
    cand_emb,
    cand_user,
    cross_down,
    cross_up,
    cross_bias,
    score_weight,
):
    devices = lax.axis_size("seq")
    history_out, user_rows = history_layer(
        devices, user_spans, user_tails, norm_gain[None, :], projected, history_in, out_proj
    )
    device_ids = jnp.arange(devices, dtype=jnp.int32)
    user_count = user_spans.shape[0]
    users = jnp.arange(user_count, dtype=jnp.int32)
    last_dev = jnp.sum(jnp.where(users[None, :] <= users[:, None], user_spans[None, :], 0), axis=1) - 1
    user_match = cand_user[:, None] == jnp.arange(user_count, dtype=jnp.int32)[None, :]
    cand_dev = jnp.sum(jnp.where(user_match, last_dev[None, :], 0), axis=1)
    selector = (cand_dev[:, None] == device_ids[None, :]).astype(jnp.bfloat16)
    user_part = jnp.dot(selector, user_rows, preferred_element_type=jnp.float32).astype(
        jnp.bfloat16
    )
    crossed_in = jnp.concatenate([user_part, cand_emb], axis=1)
    low_rank = jnp.dot(crossed_in, cross_down, preferred_element_type=jnp.float32).astype(
        jnp.bfloat16
    )
    up_part = jnp.dot(low_rank, cross_up, preferred_element_type=jnp.float32)
    input_float = crossed_in.astype(jnp.float32)
    crossed = input_float * (up_part + cross_bias) + input_float
    scores = jnp.sum(crossed * score_weight, axis=1)
    return (history_out, scores)


def solution(mesh):
    in_specs = (
        P(("rep", "seq"), None),
        P(("rep", "seq"), None),
        P(),
        P(),
        P("rep"),
        P("rep"),
        P(("rep", "seq"), None),
        P(("rep", "seq")),
        P(),
        P(),
        P(),
        P(),
    )
    out_specs = (P(("rep", "seq"), None), P(("rep", "seq")))
    return jax.shard_map(body, mesh=mesh, in_specs=in_specs, out_specs=out_specs, check_vma=False)
```

```python
import functools

import jax
import jax.numpy as jnp
from jax import lax
from jax.experimental import pallas as pl
from jax.experimental.pallas import tpu as pltpu
from jax.sharding import PartitionSpec as P

HEADS = 8
LAG = 3
OWN_FROM = 3
MESH = pl.DeviceIdType.MESH
OWN, PAIR = range(2)
TO_PAIR, TO_NEAR, TO_FAR, PART, RELAY, PASS, ROW = range(7)
QUERIES, FILLS, GATES, RESIDUAL, WEIGHTS, ROWS, OUT, USERS, CAND, DOWN, UP, BIAS, SCORE, SCORES = range(14)


def history_kernel(
    n, row_tile, spans_ref, tails_ref, gain_ref, proj_ref, hist_ref, weight_ref, user_ref, cand_ref, down_ref, up_ref, bias_ref, score_ref,
    out_ref, scores_ref,
    kv, queries, gates, residual, weights, attn, final_row, in1, in2, in3, in4, in5, out1, out2,
    rows_in, out_tile, cand_user, cand, down, up, bias, score_weight, scores, last_query, asked, answers, answer, answered,
    load_sem, once_sem, send_sem, pair_recv, recv1, recv2, recv3, recv4, recv5,
    ask_send, ask_recv, answer_send, answer_recv,
):
    rep, me = lax.axis_index("rep"), lax.axis_index("seq")
    core = lax.rem(me, 2)
    side = lax.rem(me // 2, 2)
    rows, width = residual.shape
    size = width // HEADS
    half_scale = 0.5 * size ** (-0.5)
    tiles = rows // row_tile
    steps = HEADS * tiles
    partner = me + 1 - 2 * core
    even, odd = core == 0, core == 1
    slot_a, slot_b = odd & (side == 0), odd & (side == 1)

    def dev(shift):
        return lax.rem(me + shift + n, n)

    def columns(part, h):
        return pl.ds(pl.multiple_of(part * width + h * size, size), size)

    def load(h, part, target, sem):
        return pltpu.make_async_copy(proj_ref.at[:, columns(part, h)], target, sem)

    def load_queries(h, tile, target, sem):
        block = proj_ref.at[pl.ds(tile * row_tile, row_tile), columns(1, h)]
        return pltpu.make_async_copy(block, target, sem)

    def loads(h):
        return (
            load(h, 2, kv.at[OWN, h, 0], load_sem.at[h]),
            load(h, 3, kv.at[OWN, h, 1], load_sem.at[h]),
        )

    def query_load(h, tile):
        s = tile * HEADS + h
        return load_queries(h, tile, queries.at[s], once_sem.at[QUERIES])

    late = (
        pltpu.make_async_copy(proj_ref.at[:, pl.ds(0, width)], gates, once_sem.at[GATES]),
        pltpu.make_async_copy(hist_ref, residual, once_sem.at[RESIDUAL]),
        pltpu.make_async_copy(weight_ref, weights, once_sem.at[WEIGHTS]),
    )
    side_loads = (
        pltpu.make_async_copy(user_ref, cand_user, once_sem.at[USERS]),
        pltpu.make_async_copy(cand_ref, cand, once_sem.at[CAND]),
        pltpu.make_async_copy(down_ref, down, once_sem.at[DOWN]),
        pltpu.make_async_copy(up_ref, up, once_sem.at[UP]),
        pltpu.make_async_copy(bias_ref, bias, once_sem.at[BIAS]),
        pltpu.make_async_copy(score_ref, score_weight, once_sem.at[SCORE]),
    )
    scores_out = pltpu.make_async_copy(scores, scores_ref, once_sem.at[SCORES])
    fills = [load_queries(s % HEADS, s // HEADS, out1.at[s], once_sem.at[FILLS]) for s in range(LAG)]
    fill_here = slot_b | (slot_a & (me + 4 >= n))

    @pl.when(fill_here)
    def _():
        for copy in fills:
            copy.start()

    for tile in range(tiles):
        @pl.loop(0, HEADS)
        def _(h):
            query_load(h, tile).start()

    @pl.loop(0, HEADS)
    def _(h):
        for copy in loads(h):
            copy.start()

    for copy in late + side_loads:
        copy.start()

    asked[...] = jnp.zeros_like(asked)
    answered[...] = jnp.zeros_like(answered)

    barrier = pltpu.get_barrier_semaphore()

    @pl.loop(1, n)
    def _(shift):
        pl.semaphore_signal(
            barrier, inc=1, device_id=(rep, dev(shift)), device_id_type=MESH
        )

    seen = (me, me + 1, me + 2, me + 3, me + 4, 4 * (me // 4) + 5)

    def scan_user(user, found):
        start, last, tail, firsts = found
        end = start + spans_ref[user]
        mine = (start <= me) & (me < end)
        return (
            end,
            jnp.where(mine, end - 1, last),
            jnp.where(mine, tails_ref[user], tail),
            tuple(
                jnp.where((start <= s) & (s < end), start, first) for s, first in zip(seen, firsts)
            ),
        )

    zero = jnp.int32(0)
    _, last, tail, firsts = lax.fori_loop(
        0, spans_ref.shape[0], scan_user, (zero, zero, zero, (jnp.int32(2 * n),) * len(seen))
    )
    valid = jnp.where(me == last, tail, rows)
    first_me, first_near, first_far, first_slot = firsts[0], firsts[2], firsts[4], firsts[5]
    final = jnp.clip(valid - 1, 0, rows - 1)
    swapped = first_slot <= 4 * (me // 4) + 3

    pl.semaphore_wait(barrier, n - 1)

    def remote(source, target, send_sem, recv_sem, device):
        return pltpu.make_async_remote_copy(
            src_ref=source,
            dst_ref=target,
            send_sem=send_sem,
            recv_sem=recv_sem,
            device_id=(rep, device),
            device_id_type=MESH,
        )

    def all_here(block, sem):
        pltpu.make_async_copy(block, block, sem).wait()

    def pair(h):
        return remote(kv.at[OWN, h], kv.at[PAIR, h], send_sem.at[TO_PAIR], pair_recv.at[h], partner)

    def near(s):
        return remote(queries.at[s], in1.at[s], send_sem.at[TO_NEAR], recv1.at[s], dev(-2))

    def far(s):
        return remote(queries.at[s], in2.at[s], send_sem.at[TO_FAR], recv2.at[s], dev(-4))

    def across(s):
        return remote(queries.at[s], in5.at[s], send_sem.at[TO_NEAR], recv5.at[s], dev(2))

    def onward(s):
        return remote(in5.at[s], in1.at[s], send_sem.at[PASS], recv1.at[s], dev(-4))

    def far_first(s):
        return remote(queries.at[s], out1.at[s], send_sem.at[TO_FAR], recv2.at[s], dev(-4))

    def near_sum(s):
        return remote(out1.at[s], in3.at[s], send_sem.at[PART], recv3.at[s // HEADS], dev(2))

    def far_sum(s):
        return remote(out2.at[s], in4.at[s], send_sem.at[RELAY], recv4.at[s // HEADS], dev(4))

    def slot(t):
        other = me + 2 - 4 * side
        return remote(out1.at[t], in1.at[t], send_sem.at[PART], recv1.at[t], other)

    def relay(t):
        return remote(in1.at[t], in3.at[t], send_sem.at[RELAY], recv3.at[jnp.maximum(t - LAG, 0) // HEADS], dev(4))

    def ask(back):
        return remote(last_query, asked.at[back], ask_send.at[back], ask_recv.at[back], dev(-back))

    def reply(ahead):
        return remote(answer.at[ahead], answered.at[ahead], answer_send.at[ahead], answer_recv.at[ahead], dev(ahead))

    def row_to(shift):
        return remote(final_row, rows_in.at[me], send_sem.at[ROW], once_sem.at[ROWS], dev(shift))

    def at_last(low, count):
        hit = low + lax.broadcasted_iota(jnp.int32, (16, count), 1) == final
        return jnp.where(hit, 1.0, 0.0).astype(jnp.bfloat16)

    all_here(queries, once_sem.at[QUERIES])

    def send_queries(begin, end):
        @pl.loop(begin, end)
        def _(s):
            @pl.when(even & (side == 1))
            def _():
                near(s).start()

            @pl.when(even & (side == 0) & (me >= 4))
            def _():
                across(s).start()
                far(s).start()

            @pl.when(slot_a & (me >= 4))
            def _():
                @pl.when(s < LAG)
                def _():
                    far_first(s).start()

                @pl.when(s >= LAG)
                def _():
                    far(s).start()

    send_queries(0, 2)

    @pl.loop(0, HEADS)
    def _(h):
        row = sum(
            jnp.dot(
                at_last(tile * row_tile, row_tile), queries[tile * HEADS + h],
                preferred_element_type=jnp.float32,
            )
            for tile in range(tiles)
        )
        last_query[:, pl.ds(pl.multiple_of(h * size, size), size)] = row[0:1]

    asked[0] = last_query[...]

    @pl.loop(0, HEADS)
    def _(h):
        all_here(kv.at[OWN, h], load_sem.at[h])
        pair(h).start()

    for back in (1, 2, 3):
        pl.when(me >= back)(ask(back).start)

    send_queries(2, steps)

    def weigh(q, k):
        half = half_scale * lax.dot_general(
            q, k, (((1,), (1,)), ((), ())), preferred_element_type=jnp.float32
        )
        return half + half * jnp.tanh(half)

    causal = lax.broadcasted_iota(jnp.int32, (row_tile, row_tile), 1) <= (
        lax.broadcasted_iota(jnp.int32, (row_tile, row_tile), 0)
    )

    def head_columns(h):
        return pl.ds(pl.multiple_of(h * size, size), size)

    def over(q, which, h, wanted):
        w = weigh(q, kv[which, h, 0]).astype(jnp.bfloat16)
        part = jnp.dot(w, kv[which, h, 1], preferred_element_type=jnp.float32)
        return jnp.where(wanted, part, 0.0)

    def ask_phase(at):
        @pl.when(at == 2)
        def _():
            for ahead in (1, 2, 3):
                pl.when(me + ahead < n)(ask(ahead).wait_recv)
            visible = (lax.broadcasted_iota(jnp.int32, (8, rows), 0) > 0) | (
                lax.broadcasted_iota(jnp.int32, (8, rows), 1) <= final
            )

            @pl.loop(0, HEADS)
            def _(h):
                q = asked[:, 0, head_columns(h)].astype(jnp.bfloat16)
                w = jnp.where(visible, weigh(q, kv[OWN, h, 0]), 0.0).astype(jnp.bfloat16)
                answers[:, head_columns(h)] = jnp.dot(
                    w, kv[OWN, h, 1], preferred_element_type=jnp.float32
                )

            for ahead in (1, 2, 3):
                answer[ahead] = jnp.where(firsts[ahead] <= me, answers[ahead:ahead + 1], 0.0)

        @pl.when(at == 3)
        def _():
            for ahead in (1, 2, 3):
                pl.when(me + ahead < n)(reply(ahead).start)

    gain = gain_ref[...]

    def finish(x, gate, rest):
        centered = x - jnp.mean(x, axis=1, keepdims=True)
        var = jnp.mean(centered * centered, axis=1, keepdims=True)
        normed = centered * lax.rsqrt(var + 1e-06) * gain
        gated = (normed * gate.astype(jnp.float32)).astype(jnp.bfloat16)
        out = jnp.dot(gated, weights[...], preferred_element_type=jnp.float32)
        return (out + rest.astype(jnp.float32)).astype(jnp.bfloat16)

    def row_phase(at):
        @pl.when(at == 0)
        def _():
            for copy in late:
                copy.wait()
            for back in (1, 2, 3):
                pl.when(me >= back)(reply(back).wait_recv)
            total = answers[0:1] + answered[1] + answered[2] + answered[3]
            pick = at_last(0, rows)
            row = finish(
                jnp.broadcast_to(total, (16, width)),
                jnp.dot(pick, gates[...], preferred_element_type=jnp.float32),
                jnp.dot(pick, residual[...], preferred_element_type=jnp.float32),
            ).astype(jnp.float32)[0:1]
            final_row[...] = row
            rows_in[me] = row

        @pl.when(at == 1)
        def _():
            @pl.loop(1, n)
            def _(shift):
                row_to(shift).start()

    def own(h, tile):
        low, high = tile * row_tile, (tile + 1) * row_tile
        q = queries[tile * HEADS + h]
        edge = jnp.where(causal, weigh(q, kv[OWN, h, 0, low:high]), 0.0).astype(jnp.bfloat16)
        total = jnp.dot(edge, kv[OWN, h, 1, low:high], preferred_element_type=jnp.float32)
        if tile:
            full = weigh(q, kv[OWN, h, 0, :low]).astype(jnp.bfloat16)
            total += jnp.dot(full, kv[OWN, h, 1, :low], preferred_element_type=jnp.float32)
        return total

    def add(h, tile, part):
        low, high = tile * row_tile, (tile + 1) * row_tile
        attn[low:high, head_columns(h)] += part.astype(jnp.float32)

    mine = first_me <= me - 2

    def gather(tile):
        @pl.when(even & (me >= 4))
        def _():
            all_here(in4.at[pl.ds(tile * HEADS, HEADS)], recv4.at[tile])

            @pl.loop(0, HEADS)
            def _(h):
                add(h, tile, in4[tile * HEADS + h])

        @pl.when(even & (me >= 2))
        def _():
            all_here(in3.at[pl.ds(tile * HEADS, HEADS)], recv3.at[tile])

            @pl.loop(0, HEADS)
            def _(h):
                add(h, tile, in3[tile * HEADS + h])

        @pl.when(slot_b)
        def _():
            @pl.loop(0, HEADS)
            def _(h):
                add(h, tile, jnp.where(mine, in1[tile * HEADS + h + LAG], 0.0))

        @pl.when(slot_a & (me >= 4))
        def _():
            if tile == 0:
                all_here(in3.at[pl.ds(0, HEADS + LAG)], recv3.at[0])
            else:
                all_here(in3.at[pl.ds(tile * HEADS + LAG, HEADS)], recv3.at[tile])

            @pl.loop(0, HEADS)
            def _(h):
                add(h, tile, jnp.where(mine, in3[tile * HEADS + h + LAG], 0.0))

    def write(low, high, sem):
        return pltpu.make_async_copy(out_tile.at[pl.ds(low, high - low)], out_ref.at[pl.ds(low, high - low)], sem)

    parts = [(tile * row_tile, (tile + 1) * row_tile) for tile in range(tiles - 1)]
    cut = (tiles - 1) * row_tile + row_tile // 2 // 16 * 16
    parts += [(low, high) for low, high in (((tiles - 1) * row_tile, cut), (cut, rows)) if low < high]

    def close(part):
        low, high = parts[part]
        ids = low + lax.broadcasted_iota(jnp.int32, (high - low, 1), 0)
        x = jnp.where(ids < valid, attn[low:high], 0.0)
        out_tile[low:high] = finish(x, gates[low:high], residual[low:high])
        write(low, high, once_sem.at[OUT]).start()

    def close_early():
        for tile in range(tiles - 1):
            gather(tile)
            close(tile)

    def score():
        for copy in side_loads:
            copy.wait()
        all_here(rows_in.at[pl.ds(0, n - 1)], once_sem.at[ROWS])
        count = cand.shape[0]
        device = lax.broadcasted_iota(jnp.int32, (n, count), 0)
        users = cand_user[...]

        def pick_user(user, found):
            start, chosen = found
            end = start + spans_ref[user]
            return end, jnp.where((users == user) & (device == end - 1), 1.0, chosen)

        _, chosen = lax.fori_loop(
            0, spans_ref.shape[0], pick_user, (zero, jnp.zeros((n, count), jnp.float32))
        )
        user_part = lax.dot_general(
            chosen.astype(jnp.bfloat16), rows_in[:, 0, :].astype(jnp.bfloat16),
            (((0,), (0,)), ((), ())), preferred_element_type=jnp.float32,
        ).astype(jnp.bfloat16)
        low_rank = jnp.dot(user_part, down[:width], preferred_element_type=jnp.float32)
        low_rank += jnp.dot(cand[...], down[width:], preferred_element_type=jnp.float32)
        low_rank = low_rank.astype(jnp.bfloat16)
        total = jnp.zeros((count, 1), jnp.float32)
        for half, source in ((0, user_part), (1, cand[...])):
            span = slice(half * width, (half + 1) * width)
            up_part = jnp.dot(low_rank, up[:, span], preferred_element_type=jnp.float32)
            value = source.astype(jnp.float32)
            crossed = value * (up_part + bias[:, span]) + value
            total += jnp.sum(crossed * score_weight[:, span], axis=1, keepdims=True)
        diagonal = lax.broadcasted_iota(jnp.int32, (count, count), 0) == (
            lax.broadcasted_iota(jnp.int32, (count, count), 1)
        )
        scores[...] = jnp.sum(jnp.where(diagonal, total, 0.0), axis=0, keepdims=True)
        scores_out.start()

    @pl.when(even)
    def _():
        for tile in range(tiles):
            @pl.loop(0, HEADS)
            def _(h):
                s = tile * HEADS + h
                if tile == 0:
                    ask_phase(h)
                if tile == tiles - 1:
                    row_phase(h - HEADS + 2)

                @pl.when((side == 1) & (me >= 4))
                def _():
                    across(s).wait_recv()
                    onward(s).start()
                    far(s).start()

                attn[tile * row_tile:(tile + 1) * row_tile, head_columns(h)] = own(h, tile)

                @pl.when((s >= 1) & (me + 2 < n))
                def _():
                    near_sum(s - 1).start()

                @pl.when((s >= 1) & (me + 4 < n))
                def _():
                    far_sum(s - 1).start()

                if tile == 0:
                    pair(h).wait_recv()

                @pl.when(me + 2 < n)
                def _():
                    near(s).wait_recv()
                    q = in1[s]
                    total = over(q, OWN, h, first_near <= me)
                    total += over(q, PAIR, h, first_near <= me + 1)
                    out1[s] = total.astype(jnp.bfloat16)

                @pl.when(me + 4 < n)
                def _():
                    far(s).wait_recv()
                    out2[s] = over(in2[s], PAIR, h, first_far <= me + 1).astype(jnp.bfloat16)

        @pl.when(me + 2 < n)
        def _():
            near_sum(steps - 1).start()

        @pl.when(me + 4 < n)
        def _():
            far_sum(steps - 1).start()

        close_early()
        score()

    @pl.when(odd)
    def _():
        @pl.when(fill_here)
        def _():
            all_here(out1.at[pl.ds(0, LAG)], once_sem.at[FILLS])

        @pl.when(slot_a & (me + 4 < n))
        def _():
            for s in range(LAG):
                far_first(s).wait_recv()

        for t in range(LAG):
            slot(t).start()

        def pass_on(t):
            slot(t).wait_recv()

            @pl.when((side == 0) & (me + 4 < n))
            def _():
                relay(t).start()

        begin = min(OWN_FROM, steps - HEADS)

        @pl.loop(0, steps)
        def _(t):
            h = lax.rem(t, HEADS)

            @pl.when(t < HEADS)
            def _():
                pair(h).wait_recv()

            ask_phase(t)
            row_phase(t - steps + HEADS - HEADS // 2)
            pass_on(t)

            @pl.when(t >= 1)
            def _():
                slot(t + LAG - 1).start()

            q = in1[t]
            total = over(q, OWN, h, first_near <= me)
            total += over(q, PAIR, h, first_near <= me - 1)
            out1[t + LAG] = total.astype(jnp.bfloat16)

            @pl.when((t + LAG < steps) & (side == 1))
            def _():
                out1[t + LAG] = jnp.where(swapped, out1[t + LAG], queries[t + LAG])

            @pl.when((t + LAG < steps) & (side == 0) & (me + 4 < n))
            def _():
                far(t + LAG).wait_recv()
                out1[t + LAG] = jnp.where(swapped, in2[t + LAG], out1[t + LAG])

            @pl.when((t >= begin) & (t < begin + HEADS))
            def _():
                mine_h = t - begin
                for tile in range(tiles):
                    attn[tile * row_tile:(tile + 1) * row_tile, head_columns(mine_h)] = own(
                        mine_h, tile
                    ) + over(queries[tile * HEADS + mine_h], PAIR, mine_h, first_me <= me - 1)

        slot(steps + LAG - 1).start()
        pass_on(steps)
        close_early()

        @pl.loop(steps + 1, steps + LAG - 1)
        def _(t):
            pass_on(t)

        score()
        pass_on(steps + LAG - 1)

    gather(tiles - 1)

    for part in range(tiles - 1, len(parts)):
        close(part)

    all_here(kv.at[OWN], send_sem.at[TO_PAIR])

    @pl.when(even & ((side == 1) | (me >= 4)))
    def _():
        all_here(queries, send_sem.at[TO_NEAR])

    @pl.when((even | slot_a) & (me >= 4))
    def _():
        all_here(queries, send_sem.at[TO_FAR])

    @pl.when(even & (side == 1) & (me >= 4))
    def _():
        all_here(in5, send_sem.at[PASS])

    @pl.when(even & (me + 2 < n))
    def _():
        all_here(out1.at[pl.ds(0, steps)], send_sem.at[PART])

    @pl.when(even & (me + 4 < n))
    def _():
        all_here(out2, send_sem.at[RELAY])

    @pl.when(odd)
    def _():
        all_here(out1, send_sem.at[PART])

    @pl.when(slot_a & (me + 4 < n))
    def _():
        all_here(in1, send_sem.at[RELAY])

    for back in (1, 2, 3):
        pl.when(me >= back)(ask(back).wait_send)
        pl.when(me + back < n)(reply(back).wait_send)

    all_here(rows_in.at[pl.ds(0, n - 1)], send_sem.at[ROW])
    scores_out.wait()
    all_here(out_tile, once_sem.at[OUT])


def history_layer(
    n, spans, tails, gain, projected, history_in, out_proj, cand_user, cand_emb, cross_down, cross_up, cross_bias, score_weight
):
    rows, width = history_in.shape
    size = width // HEADS
    row_tile = next(t for t in (384, 256, 128, 64, 32, 16, rows) if rows % t == 0)
    steps = HEADS * (rows // row_tile)
    slots = steps + LAG
    smem = pl.BlockSpec(memory_space=pltpu.SMEM)
    anywhere = pl.BlockSpec(memory_space=pl.ANY)
    vmem = pl.BlockSpec(memory_space=pltpu.VMEM)
    blocks = lambda count: pltpu.VMEM((count, row_tile, size), jnp.bfloat16)
    dma = lambda *shape: pltpu.SemaphoreType.DMA(shape)
    return pl.pallas_call(
        functools.partial(history_kernel, n, row_tile),
        out_shape=(
            jax.ShapeDtypeStruct((rows, width), jnp.bfloat16),
            jax.ShapeDtypeStruct(cand_user.shape, jnp.float32),
        ),
        in_specs=[smem, smem, vmem] + [anywhere] * 9,
        out_specs=(anywhere, anywhere),
        scratch_shapes=[
            pltpu.VMEM((2, HEADS, 2, rows, size), jnp.bfloat16),
            blocks(steps),
            pltpu.VMEM((rows, width), jnp.bfloat16),
            pltpu.VMEM((rows, width), jnp.bfloat16),
            pltpu.VMEM((width, width), jnp.bfloat16),
            pltpu.VMEM((rows, width), jnp.float32),
            pltpu.VMEM((1, width), jnp.float32),
            blocks(slots),
            blocks(steps),
            blocks(slots),
            blocks(steps),
            blocks(steps),
            blocks(slots),
            blocks(steps),
            pltpu.VMEM((n, 1, width), jnp.float32),
            pltpu.VMEM((rows, width), jnp.bfloat16),
            pltpu.VMEM(cand_user.shape, jnp.int32),
            pltpu.VMEM(cand_emb.shape, jnp.bfloat16),
            pltpu.VMEM(cross_down.shape, jnp.bfloat16),
            pltpu.VMEM(cross_up.shape, jnp.bfloat16),
            pltpu.VMEM(cross_bias.shape, jnp.float32),
            pltpu.VMEM(score_weight.shape, jnp.float32),
            pltpu.VMEM(cand_user.shape, jnp.float32),
            pltpu.VMEM((1, width), jnp.float32),
            pltpu.VMEM((8, 1, width), jnp.float32),
            pltpu.VMEM((8, width), jnp.float32),
            pltpu.VMEM((4, 1, width), jnp.float32),
            pltpu.VMEM((4, 1, width), jnp.float32),
            dma(HEADS),
            dma(14),
            dma(7),
            dma(HEADS),
            dma(slots),
            dma(steps),
            dma(rows // row_tile),
            dma(rows // row_tile),
            dma(steps),
            dma(4),
            dma(4),
            dma(4),
            dma(4),
        ],
        compiler_params=pltpu.CompilerParams(
            collective_id=0, has_side_effects=True, vmem_limit_bytes=60 * 1024 * 1024
        ),
        name="history_layer",
    )(
        spans, tails, gain, projected, history_in, out_proj, cand_user, cand_emb, cross_down, cross_up,
        cross_bias, score_weight,
    )


def body(
    projected,
    history_in,
    norm_gain,
    out_proj,
    user_spans,
    user_tails,
    cand_emb,
    cand_user,
    cross_down,
    cross_up,
    cross_bias,
    score_weight,
):
    history_out, scores = history_layer(
        lax.axis_size("seq"), user_spans, user_tails, norm_gain[None, :], projected, history_in, out_proj,
        cand_user[None, :], cand_emb, cross_down, cross_up, cross_bias[None, :], score_weight[None, :],
    )
    return (history_out, scores[0])


def solution(mesh):
    in_specs = (
        P(("rep", "seq"), None),
        P(("rep", "seq"), None),
        P(),
        P(),
        P("rep"),
        P("rep"),
        P(("rep", "seq"), None),
        P(("rep", "seq")),
        P(),
        P(),
        P(),
        P(),
    )
    out_specs = (P(("rep", "seq"), None), P(("rep", "seq")))
    return jax.shard_map(body, mesh=mesh, in_specs=in_specs, out_specs=out_specs, check_vma=False)
```

```python
import functools

import jax
import jax.numpy as jnp
from jax import lax
from jax.experimental import pallas as pl
from jax.experimental.pallas import tpu as pltpu
from jax.sharding import PartitionSpec as P

HEADS = 8
LAG = 3
OWN_FROM = 2
AHEAD = 2
MESH = pl.DeviceIdType.MESH
OWN, PAIR = range(2)
TO_PAIR, TO_NEAR, TO_FAR, PART, RELAY, PASS, ROW = range(7)
QUERIES, FILLS, GATES, RESIDUAL, WEIGHTS, ROWS, OUT, USERS, CAND, DOWN, UP, BIAS, SCORE, SCORES = range(14)


def history_kernel(
    n, row_tile, spans_ref, tails_ref, gain_ref, proj_ref, hist_ref, weight_ref, user_ref, cand_ref, down_ref, up_ref, bias_ref, score_ref,
    out_ref, scores_ref,
    kv, queries, gates, residual, weights, attn, final_row, in1, in2, in3, in4, in5, out1, out2,
    rows_in, out_tile, cand_user, cand, down, up, bias, score_weight, scores, last_query, asked, answers, answer, answered,
    load_sem, once_sem, send_sem, pair_recv, recv1, recv2, recv3, recv4, recv5,
    ask_send, ask_recv, answer_send, answer_recv,
):
    rep, me = lax.axis_index("rep"), lax.axis_index("seq")
    core = lax.rem(me, 2)
    side = lax.rem(me // 2, 2)
    rows, width = residual.shape
    size = width // HEADS
    half_scale = 0.5 * size ** (-0.5)
    tiles = rows // row_tile
    steps = HEADS * tiles
    partner = me + 1 - 2 * core
    even, odd = core == 0, core == 1
    slot_a, slot_b = odd & (side == 0), odd & (side == 1)

    def dev(shift):
        return lax.rem(me + shift + n, n)

    def columns(part, h):
        return pl.ds(pl.multiple_of(part * width + h * size, size), size)

    def load(h, part, target, sem):
        return pltpu.make_async_copy(proj_ref.at[:, columns(part, h)], target, sem)

    def load_queries(h, tile, target, sem):
        block = proj_ref.at[pl.ds(tile * row_tile, row_tile), columns(1, h)]
        return pltpu.make_async_copy(block, target, sem)

    def loads(h):
        return (
            load(h, 2, kv.at[OWN, h, 0], load_sem.at[h]),
            load(h, 3, kv.at[OWN, h, 1], load_sem.at[h]),
        )

    def query_load(h, tile):
        s = tile * HEADS + h
        return load_queries(h, tile, queries.at[s], once_sem.at[QUERIES])

    late = (
        pltpu.make_async_copy(proj_ref.at[:, pl.ds(0, width)], gates, once_sem.at[GATES]),
        pltpu.make_async_copy(hist_ref, residual, once_sem.at[RESIDUAL]),
        pltpu.make_async_copy(weight_ref, weights, once_sem.at[WEIGHTS]),
    )
    side_loads = (
        pltpu.make_async_copy(user_ref, cand_user, once_sem.at[USERS]),
        pltpu.make_async_copy(cand_ref, cand, once_sem.at[CAND]),
        pltpu.make_async_copy(down_ref, down, once_sem.at[DOWN]),
        pltpu.make_async_copy(up_ref, up, once_sem.at[UP]),
        pltpu.make_async_copy(bias_ref, bias, once_sem.at[BIAS]),
        pltpu.make_async_copy(score_ref, score_weight, once_sem.at[SCORE]),
    )
    scores_out = pltpu.make_async_copy(scores, scores_ref, once_sem.at[SCORES])
    fills = [load_queries(s % HEADS, s // HEADS, out1.at[s], once_sem.at[FILLS]) for s in range(LAG)]
    fill_here = slot_b | (slot_a & (me + 4 >= n))

    @pl.when(fill_here)
    def _():
        for copy in fills:
            copy.start()

    for tile in range(tiles):
        @pl.loop(0, HEADS)
        def _(h):
            query_load(h, tile).start()

    @pl.loop(0, HEADS)
    def _(h):
        for copy in loads(h):
            copy.start()

    for copy in late + side_loads:
        copy.start()

    asked[...] = jnp.zeros_like(asked)
    answered[...] = jnp.zeros_like(answered)

    barrier = pltpu.get_barrier_semaphore()

    @pl.loop(1, n)
    def _(shift):
        pl.semaphore_signal(
            barrier, inc=1, device_id=(rep, dev(shift)), device_id_type=MESH
        )

    seen = (me, me + 1, me + 2, me + 3, me + 4, 4 * (me // 4) + 5)

    def scan_user(user, found):
        start, last, tail, firsts = found
        end = start + spans_ref[user]
        mine = (start <= me) & (me < end)
        return (
            end,
            jnp.where(mine, end - 1, last),
            jnp.where(mine, tails_ref[user], tail),
            tuple(
                jnp.where((start <= s) & (s < end), start, first) for s, first in zip(seen, firsts)
            ),
        )

    zero = jnp.int32(0)
    _, last, tail, firsts = lax.fori_loop(
        0, spans_ref.shape[0], scan_user, (zero, zero, zero, (jnp.int32(2 * n),) * len(seen))
    )
    valid = jnp.where(me == last, tail, rows)
    first_me, first_near, first_far, first_slot = firsts[0], firsts[2], firsts[4], firsts[5]
    final = jnp.clip(valid - 1, 0, rows - 1)
    swapped = first_slot <= 4 * (me // 4) + 3

    pl.semaphore_wait(barrier, n - 1)

    def remote(source, target, send_sem, recv_sem, device):
        return pltpu.make_async_remote_copy(
            src_ref=source,
            dst_ref=target,
            send_sem=send_sem,
            recv_sem=recv_sem,
            device_id=(rep, device),
            device_id_type=MESH,
        )

    def all_here(block, sem):
        pltpu.make_async_copy(block, block, sem).wait()

    def pair(h):
        return remote(kv.at[OWN, h], kv.at[PAIR, h], send_sem.at[TO_PAIR], pair_recv.at[h], partner)

    def near(s):
        return remote(queries.at[s], in1.at[s], send_sem.at[TO_NEAR], recv1.at[s], dev(-2))

    def far(s):
        return remote(queries.at[s], in2.at[s], send_sem.at[TO_FAR], recv2.at[s], dev(-4))

    def across(s):
        return remote(queries.at[s], in5.at[s], send_sem.at[TO_NEAR], recv5.at[s], dev(2))

    def onward(s):
        return remote(in5.at[s], in1.at[s], send_sem.at[PASS], recv1.at[s], dev(-4))

    def far_first(s):
        return remote(queries.at[s], out1.at[s], send_sem.at[TO_FAR], recv2.at[s], dev(-4))

    def near_sum(s):
        return remote(out1.at[s], in3.at[s], send_sem.at[PART], recv3.at[s // HEADS], dev(2))

    def far_sum(s):
        return remote(out2.at[s], in4.at[s], send_sem.at[RELAY], recv4.at[s // HEADS], dev(4))

    def slot(t):
        other = me + 2 - 4 * side
        return remote(out1.at[t], in1.at[t], send_sem.at[PART], recv1.at[t], other)

    def relay(t):
        return remote(in1.at[t], in3.at[t], send_sem.at[RELAY], recv3.at[jnp.maximum(t - LAG, 0) // HEADS], dev(4))

    def ask(back):
        return remote(last_query, asked.at[back], ask_send.at[back], ask_recv.at[back], dev(-back))

    def reply(ahead):
        return remote(answer.at[ahead], answered.at[ahead], answer_send.at[ahead], answer_recv.at[ahead], dev(ahead))

    def row_to(shift):
        return remote(final_row, rows_in.at[me], send_sem.at[ROW], once_sem.at[ROWS], dev(shift))

    def at_last(low, count):
        hit = low + lax.broadcasted_iota(jnp.int32, (16, count), 1) == final
        return jnp.where(hit, 1.0, 0.0).astype(jnp.bfloat16)

    all_here(queries, once_sem.at[QUERIES])

    def send_queries(begin, end):
        @pl.loop(begin, end)
        def _(s):
            @pl.when(even & (side == 1))
            def _():
                near(s).start()

            @pl.when(even & (side == 0) & (me >= 4))
            def _():
                across(s).start()

            @pl.when(slot_a & (me >= 4))
            def _():
                @pl.when(s < LAG)
                def _():
                    far_first(s).start()

                @pl.when(s >= LAG)
                def _():
                    far(s).start()

    send_queries(0, LAG)

    @pl.loop(0, HEADS)
    def _(h):
        row = sum(
            jnp.dot(
                at_last(tile * row_tile, row_tile), queries[tile * HEADS + h],
                preferred_element_type=jnp.float32,
            )
            for tile in range(tiles)
        )
        last_query[:, pl.ds(pl.multiple_of(h * size, size), size)] = row[0:1]

    asked[0] = last_query[...]

    @pl.loop(0, HEADS)
    def _(h):
        all_here(kv.at[OWN, h], load_sem.at[h])
        pair(h).start()

    for back in (1, 2, 3):
        pl.when(me >= back)(ask(back).start)

    send_queries(LAG, steps)

    @pl.when(even & (side == 0) & (me >= 4))
    def _():
        for s in range(AHEAD):
            far(s).start()

    def weigh(q, k):
        half = half_scale * lax.dot_general(
            q, k, (((1,), (1,)), ((), ())), preferred_element_type=jnp.float32
        )
        return half + half * jnp.tanh(half)

    causal = lax.broadcasted_iota(jnp.int32, (row_tile, row_tile), 1) <= (
        lax.broadcasted_iota(jnp.int32, (row_tile, row_tile), 0)
    )

    def head_columns(h):
        return pl.ds(pl.multiple_of(h * size, size), size)

    def over(q, which, h, wanted):
        w = weigh(q, kv[which, h, 0]).astype(jnp.bfloat16)
        part = jnp.dot(w, kv[which, h, 1], preferred_element_type=jnp.float32)
        return jnp.where(wanted, part, 0.0)

    def ask_phase(at):
        @pl.when(at == 2)
        def _():
            for ahead in (1, 2, 3):
                pl.when(me + ahead < n)(ask(ahead).wait_recv)
            visible = (lax.broadcasted_iota(jnp.int32, (8, rows), 0) > 0) | (
                lax.broadcasted_iota(jnp.int32, (8, rows), 1) <= final
            )

            @pl.loop(0, HEADS)
            def _(h):
                q = asked[:, 0, head_columns(h)].astype(jnp.bfloat16)
                w = jnp.where(visible, weigh(q, kv[OWN, h, 0]), 0.0).astype(jnp.bfloat16)
                answers[:, head_columns(h)] = jnp.dot(
                    w, kv[OWN, h, 1], preferred_element_type=jnp.float32
                )

            for ahead in (1, 2, 3):
                answer[ahead] = jnp.where(firsts[ahead] <= me, answers[ahead:ahead + 1], 0.0)

        @pl.when(at == 3)
        def _():
            for ahead in (1, 2, 3):
                pl.when(me + ahead < n)(reply(ahead).start)

    gain = gain_ref[...]

    def finish(x, gate, rest):
        centered = x - jnp.mean(x, axis=1, keepdims=True)
        var = jnp.mean(centered * centered, axis=1, keepdims=True)
        normed = centered * lax.rsqrt(var + 1e-06) * gain
        gated = (normed * gate.astype(jnp.float32)).astype(jnp.bfloat16)
        out = jnp.dot(gated, weights[...], preferred_element_type=jnp.float32)
        return (out + rest.astype(jnp.float32)).astype(jnp.bfloat16)

    def row_phase(at):
        @pl.when(at == 0)
        def _():
            for copy in late:
                copy.wait()
            for back in (1, 2, 3):
                pl.when(me >= back)(reply(back).wait_recv)
            total = answers[0:1] + answered[1] + answered[2] + answered[3]
            pick = at_last(0, rows)
            row = finish(
                jnp.broadcast_to(total, (16, width)),
                jnp.dot(pick, gates[...], preferred_element_type=jnp.float32),
                jnp.dot(pick, residual[...], preferred_element_type=jnp.float32),
            ).astype(jnp.float32)[0:1]
            final_row[...] = row
            rows_in[me] = row

        @pl.when(at == 1)
        def _():
            @pl.loop(1, n)
            def _(shift):
                row_to(shift).start()

    def own(h, tile):
        low, high = tile * row_tile, (tile + 1) * row_tile
        q = queries[tile * HEADS + h]
        edge = jnp.where(causal, weigh(q, kv[OWN, h, 0, low:high]), 0.0).astype(jnp.bfloat16)
        total = jnp.dot(edge, kv[OWN, h, 1, low:high], preferred_element_type=jnp.float32)
        if tile:
            full = weigh(q, kv[OWN, h, 0, :low]).astype(jnp.bfloat16)
            total += jnp.dot(full, kv[OWN, h, 1, :low], preferred_element_type=jnp.float32)
        return total

    def add(h, tile, part):
        low, high = tile * row_tile, (tile + 1) * row_tile
        attn[low:high, head_columns(h)] += part.astype(jnp.float32)

    mine = first_me <= me - 2

    def gather(tile):
        @pl.when(even & (me >= 4))
        def _():
            all_here(in4.at[pl.ds(tile * HEADS, HEADS)], recv4.at[tile])

            @pl.loop(0, HEADS)
            def _(h):
                add(h, tile, in4[tile * HEADS + h])

        @pl.when(even & (me >= 2))
        def _():
            all_here(in3.at[pl.ds(tile * HEADS, HEADS)], recv3.at[tile])

            @pl.loop(0, HEADS)
            def _(h):
                add(h, tile, in3[tile * HEADS + h])

        @pl.when(slot_b)
        def _():
            @pl.loop(0, HEADS)
            def _(h):
                add(h, tile, jnp.where(mine, in1[tile * HEADS + h + LAG], 0.0))

        @pl.when(slot_a & (me >= 4))
        def _():
            if tile == 0:
                all_here(in3.at[pl.ds(0, HEADS + LAG)], recv3.at[0])
            else:
                all_here(in3.at[pl.ds(tile * HEADS + LAG, HEADS)], recv3.at[tile])

            @pl.loop(0, HEADS)
            def _(h):
                add(h, tile, jnp.where(mine, in3[tile * HEADS + h + LAG], 0.0))

    def write(low, high, sem):
        return pltpu.make_async_copy(out_tile.at[pl.ds(low, high - low)], out_ref.at[pl.ds(low, high - low)], sem)

    parts = [(tile * row_tile, (tile + 1) * row_tile) for tile in range(tiles - 1)]
    cut = (tiles - 1) * row_tile + row_tile // 2 // 16 * 16
    parts += [(low, high) for low, high in (((tiles - 1) * row_tile, cut), (cut, rows)) if low < high]

    def close(part):
        low, high = parts[part]
        ids = low + lax.broadcasted_iota(jnp.int32, (high - low, 1), 0)
        x = jnp.where(ids < valid, attn[low:high], 0.0)
        out_tile[low:high] = finish(x, gates[low:high], residual[low:high])
        write(low, high, once_sem.at[OUT]).start()

    def close_early():
        for tile in range(tiles - 1):
            gather(tile)
            close(tile)

    def score():
        for copy in side_loads:
            copy.wait()
        all_here(rows_in.at[pl.ds(0, n - 1)], once_sem.at[ROWS])
        count = cand.shape[0]
        device = lax.broadcasted_iota(jnp.int32, (n, count), 0)
        users = cand_user[...]

        def pick_user(user, found):
            start, chosen = found
            end = start + spans_ref[user]
            return end, jnp.where((users == user) & (device == end - 1), 1.0, chosen)

        _, chosen = lax.fori_loop(
            0, spans_ref.shape[0], pick_user, (zero, jnp.zeros((n, count), jnp.float32))
        )
        user_part = lax.dot_general(
            chosen.astype(jnp.bfloat16), rows_in[:, 0, :].astype(jnp.bfloat16),
            (((0,), (0,)), ((), ())), preferred_element_type=jnp.float32,
        ).astype(jnp.bfloat16)
        low_rank = jnp.dot(user_part, down[:width], preferred_element_type=jnp.float32)
        low_rank += jnp.dot(cand[...], down[width:], preferred_element_type=jnp.float32)
        low_rank = low_rank.astype(jnp.bfloat16)
        total = jnp.zeros((count, 1), jnp.float32)
        for half, source in ((0, user_part), (1, cand[...])):
            span = slice(half * width, (half + 1) * width)
            up_part = jnp.dot(low_rank, up[:, span], preferred_element_type=jnp.float32)
            value = source.astype(jnp.float32)
            crossed = value * (up_part + bias[:, span]) + value
            total += jnp.sum(crossed * score_weight[:, span], axis=1, keepdims=True)
        diagonal = lax.broadcasted_iota(jnp.int32, (count, count), 0) == (
            lax.broadcasted_iota(jnp.int32, (count, count), 1)
        )
        scores[...] = jnp.sum(jnp.where(diagonal, total, 0.0), axis=0, keepdims=True)
        scores_out.start()

    @pl.when(even)
    def _():
        for tile in range(tiles):
            @pl.loop(0, HEADS)
            def _(h):
                s = tile * HEADS + h
                if tile == 0:
                    ask_phase(h)
                if tile == tiles - 1:
                    row_phase(h - HEADS + 2)

                @pl.when((side == 0) & (me >= 4) & (s + AHEAD < steps))
                def _():
                    far(s + AHEAD).start()

                @pl.when((side == 1) & (me >= 4))
                def _():
                    across(s).wait_recv()
                    onward(s).start()
                    far(s).start()

                attn[tile * row_tile:(tile + 1) * row_tile, head_columns(h)] = own(h, tile)

                @pl.when((s >= 1) & (me + 2 < n))
                def _():
                    near_sum(s - 1).start()

                @pl.when((s >= 1) & (me + 4 < n))
                def _():
                    far_sum(s - 1).start()

                if tile == 0:
                    pair(h).wait_recv()

                @pl.when(me + 2 < n)
                def _():
                    near(s).wait_recv()
                    q = in1[s]
                    total = over(q, OWN, h, first_near <= me)
                    total += over(q, PAIR, h, first_near <= me + 1)
                    out1[s] = total.astype(jnp.bfloat16)

                @pl.when(me + 4 < n)
                def _():
                    far(s).wait_recv()
                    out2[s] = over(in2[s], PAIR, h, first_far <= me + 1).astype(jnp.bfloat16)

        @pl.when(me + 2 < n)
        def _():
            near_sum(steps - 1).start()

        @pl.when(me + 4 < n)
        def _():
            far_sum(steps - 1).start()

        close_early()
        score()

    @pl.when(odd)
    def _():
        @pl.when(fill_here)
        def _():
            all_here(out1.at[pl.ds(0, LAG)], once_sem.at[FILLS])

        for t in range(LAG):
            @pl.when(slot_a & (me + 4 < n))
            def _():
                far_first(t).wait_recv()

            slot(t).start()

        def pass_on(t):
            slot(t).wait_recv()

            @pl.when((side == 0) & (me + 4 < n))
            def _():
                relay(t).start()

        begin = min(OWN_FROM, steps - HEADS)

        @pl.loop(0, steps)
        def _(t):
            h = lax.rem(t, HEADS)

            @pl.when(t < HEADS)
            def _():
                pair(h).wait_recv()

            ask_phase(t)
            row_phase(t - steps + HEADS - HEADS // 2)
            pass_on(t)

            @pl.when(t >= 1)
            def _():
                slot(t + LAG - 1).start()

            q = in1[t]
            total = over(q, OWN, h, first_near <= me)
            total += over(q, PAIR, h, first_near <= me - 1)
            out1[t + LAG] = total.astype(jnp.bfloat16)

            @pl.when((t + LAG < steps) & (side == 1))
            def _():
                out1[t + LAG] = jnp.where(swapped, out1[t + LAG], queries[t + LAG])

            @pl.when((t + LAG < steps) & (side == 0) & (me + 4 < n))
            def _():
                far(t + LAG).wait_recv()
                out1[t + LAG] = jnp.where(swapped, in2[t + LAG], out1[t + LAG])

            @pl.when((t >= begin) & (t < begin + HEADS))
            def _():
                mine_h = t - begin
                for tile in range(tiles):
                    attn[tile * row_tile:(tile + 1) * row_tile, head_columns(mine_h)] = own(
                        mine_h, tile
                    ) + over(queries[tile * HEADS + mine_h], PAIR, mine_h, first_me <= me - 1)

        slot(steps + LAG - 1).start()
        pass_on(steps)
        relays = (side == 0) & (me + 4 < n)

        @pl.when(relays)
        def _():
            @pl.loop(steps + 1, steps + LAG)
            def _(t):
                pass_on(t)

        close_early()
        score()

        @pl.when(~relays)
        def _():
            @pl.loop(steps + 1, steps + LAG)
            def _(t):
                pass_on(t)

    gather(tiles - 1)

    for part in range(tiles - 1, len(parts)):
        close(part)

    all_here(kv.at[OWN], send_sem.at[TO_PAIR])

    @pl.when(even & ((side == 1) | (me >= 4)))
    def _():
        all_here(queries, send_sem.at[TO_NEAR])

    @pl.when((even | slot_a) & (me >= 4))
    def _():
        all_here(queries, send_sem.at[TO_FAR])

    @pl.when(even & (side == 1) & (me >= 4))
    def _():
        all_here(in5, send_sem.at[PASS])

    @pl.when(even & (me + 2 < n))
    def _():
        all_here(out1.at[pl.ds(0, steps)], send_sem.at[PART])

    @pl.when(even & (me + 4 < n))
    def _():
        all_here(out2, send_sem.at[RELAY])

    @pl.when(odd)
    def _():
        all_here(out1, send_sem.at[PART])

    @pl.when(slot_a & (me + 4 < n))
    def _():
        all_here(in1, send_sem.at[RELAY])

    for back in (1, 2, 3):
        pl.when(me >= back)(ask(back).wait_send)
        pl.when(me + back < n)(reply(back).wait_send)

    all_here(rows_in.at[pl.ds(0, n - 1)], send_sem.at[ROW])
    scores_out.wait()
    all_here(out_tile, once_sem.at[OUT])


def history_layer(
    n, spans, tails, gain, projected, history_in, out_proj, cand_user, cand_emb, cross_down, cross_up, cross_bias, score_weight
):
    rows, width = history_in.shape
    size = width // HEADS
    row_tile = next(t for t in (384, 256, 128, 64, 32, 16, rows) if rows % t == 0)
    steps = HEADS * (rows // row_tile)
    slots = steps + LAG
    smem = pl.BlockSpec(memory_space=pltpu.SMEM)
    anywhere = pl.BlockSpec(memory_space=pl.ANY)
    vmem = pl.BlockSpec(memory_space=pltpu.VMEM)
    blocks = lambda count: pltpu.VMEM((count, row_tile, size), jnp.bfloat16)
    dma = lambda *shape: pltpu.SemaphoreType.DMA(shape)
    return pl.pallas_call(
        functools.partial(history_kernel, n, row_tile),
        out_shape=(
            jax.ShapeDtypeStruct((rows, width), jnp.bfloat16),
            jax.ShapeDtypeStruct(cand_user.shape, jnp.float32),
        ),
        in_specs=[smem, smem, vmem] + [anywhere] * 9,
        out_specs=(anywhere, anywhere),
        scratch_shapes=[
            pltpu.VMEM((2, HEADS, 2, rows, size), jnp.bfloat16),
            blocks(steps),
            pltpu.VMEM((rows, width), jnp.bfloat16),
            pltpu.VMEM((rows, width), jnp.bfloat16),
            pltpu.VMEM((width, width), jnp.bfloat16),
            pltpu.VMEM((rows, width), jnp.float32),
            pltpu.VMEM((1, width), jnp.float32),
            blocks(slots),
            blocks(steps),
            blocks(slots),
            blocks(steps),
            blocks(steps),
            blocks(slots),
            blocks(steps),
            pltpu.VMEM((n, 1, width), jnp.float32),
            pltpu.VMEM((rows, width), jnp.bfloat16),
            pltpu.VMEM(cand_user.shape, jnp.int32),
            pltpu.VMEM(cand_emb.shape, jnp.bfloat16),
            pltpu.VMEM(cross_down.shape, jnp.bfloat16),
            pltpu.VMEM(cross_up.shape, jnp.bfloat16),
            pltpu.VMEM(cross_bias.shape, jnp.float32),
            pltpu.VMEM(score_weight.shape, jnp.float32),
            pltpu.VMEM(cand_user.shape, jnp.float32),
            pltpu.VMEM((1, width), jnp.float32),
            pltpu.VMEM((8, 1, width), jnp.float32),
            pltpu.VMEM((8, width), jnp.float32),
            pltpu.VMEM((4, 1, width), jnp.float32),
            pltpu.VMEM((4, 1, width), jnp.float32),
            dma(HEADS),
            dma(14),
            dma(7),
            dma(HEADS),
            dma(slots),
            dma(steps),
            dma(rows // row_tile),
            dma(rows // row_tile),
            dma(steps),
            dma(4),
            dma(4),
            dma(4),
            dma(4),
        ],
        compiler_params=pltpu.CompilerParams(
            collective_id=0, has_side_effects=True, vmem_limit_bytes=60 * 1024 * 1024
        ),
        name="history_layer",
    )(
        spans, tails, gain, projected, history_in, out_proj, cand_user, cand_emb, cross_down, cross_up,
        cross_bias, score_weight,
    )


def body(
    projected,
    history_in,
    norm_gain,
    out_proj,
    user_spans,
    user_tails,
    cand_emb,
    cand_user,
    cross_down,
    cross_up,
    cross_bias,
    score_weight,
):
    history_out, scores = history_layer(
        lax.axis_size("seq"), user_spans, user_tails, norm_gain[None, :], projected, history_in, out_proj,
        cand_user[None, :], cand_emb, cross_down, cross_up, cross_bias[None, :], score_weight[None, :],
    )
    return (history_out, scores[0])


def solution(mesh):
    in_specs = (
        P(("rep", "seq"), None),
        P(("rep", "seq"), None),
        P(),
        P(),
        P("rep"),
        P("rep"),
        P(("rep", "seq"), None),
        P(("rep", "seq")),
        P(),
        P(),
        P(),
        P(),
    )
    out_specs = (P(("rep", "seq"), None), P(("rep", "seq")))
    return jax.shard_map(body, mesh=mesh, in_specs=in_specs, out_specs=out_specs, check_vma=False)
```
